256 devices in a mesh: leaf: 64 (over z, x, y_lo), panel: 4 (over y_hi, core).
Axes of the slice: x: 4, y: 4 (y_hi: 2, y_lo: 2; y = y_hi * 2 + y_lo), z: 8, core: 2. Of those that a mesh axis runs over, the one named last changes fastest.
Arguments:
- pix_cycle: bfloat16 [65536, 1536], P('leaf', 'panel'), may hold values from -6 to 6
- cycle_to_dissection: int32 [65536], replicated, may hold values from 0 to 65535, as said below
- subtree_of: int32 [64], replicated, may hold values from 0 to 63, each once
- fill_blocks: int32 [512, 12], replicated, may hold values 0 or 1
- leaf_shift: float32 [64, 1536], replicated, may hold values from 0.5 to 4
- separator_shift: float32 [1024], P('panel'), may hold values from 0.5 to 4
Outputs:
- leaf_factor: float32 [32768, 512], P('leaf', 'panel')
- leaf_coupling: float32 [65536, 512], P('leaf', 'panel')
- separator_factor: float32 [1024, 1024], P('leaf', 'panel')
The draws below stay inside these ranges and needn't reach their ends.
Inputs may be any that keep to these rules, and one draw needn't show every extreme that they name: `cycle_to_dissection`: for every subtree t, positions t * 1024 to (t + 1) * 1024 - 1 name each cycle index of the form q * 1024 + t * 16 + o, with 0 <= o < 16 and 0 <= q < 64, exactly once.
All inputs are finite; a program needn't handle non-finite values.
Results may differ from the reference program's by a relative error of at most 0.0003.
Values may be sent and summed in bfloat16 or wider, within the bound.
A program may use at most 128 MiB of HBM per device.

```python
import math
import jax
import jax.numpy as jnp
from jax import lax

ROWS = 1024
KSUP = 512
SSEP = 1024
BLK = 128
FRONT = 1536
SUBTREES = 64
NPIX = 65536
ROWBLOCKS = 8
COLBLOCKS = 12
N_LEAF = 64


def draw_cycle_to_dissection(key, part):
    block_rows = ROWS // N_LEAF
    subtree = jnp.arange(N_LEAF, dtype=jnp.int32)[:, None]
    column = jnp.arange(ROWS, dtype=jnp.int32)[None, :]
    owner = column // block_rows
    offset = column % block_rows
    base = owner * ROWS + subtree * block_rows + offset
    keys = jax.random.split(jax.random.fold_in(key, 7), N_LEAF)
    shuffled = jax.vmap(lambda single, row: jax.random.permutation(single, row))(keys, base)
    return shuffled.reshape(-1).astype(jnp.int32)


def touch_ends(entries, stream_key, smallest, largest):
    spot = [jax.random.randint(jax.random.fold_in(stream_key, axis), (), 0, length) for axis, length in enumerate(entries.shape)]
    widest = entries.shape.index(max(entries.shape))
    next_to = spot[:widest] + [(spot[widest] + 1) % entries.shape[widest]] + spot[widest + 1:]
    return entries.at[tuple(spot)].set(smallest).at[tuple(next_to)].set(largest)


def level_of(key, shape, cuts, smallest, top_value):
    loudness, own = 1.0, jax.random.fold_in(key, 6)
    for axis_at, parts in cuts:
        draws = jnp.exp(jax.random.uniform(jax.random.fold_in(own, axis_at), (parts,), jnp.float32, smallest / len(cuts), top_value / len(cuts)))
        loudness = loudness * jnp.repeat(draws, shape[axis_at] // parts).reshape([-1 if axis == axis_at else 1 for axis in range(len(shape))])
    return loudness


def centred(stream_key, shape, scale, limit, shards=(), kind=jnp.bfloat16):
    factor_of = level_of(stream_key, shape, shards, -0.22, 0.18) if shards else 1.0
    array = jax.random.normal(stream_key, shape, jnp.float32) * scale * factor_of
    return jnp.minimum(jnp.maximum(array, -limit), limit).astype(kind)


def setup_inputs(seed: int = 0) -> dict:
    seeds = jax.random.split(jax.random.key(seed), 7)
    return {
        "pix_cycle": centred(seeds[0], (NPIX, FRONT), 1.0, 6.0, ((0, 64), (1, 4))),
        "cycle_to_dissection": draw_cycle_to_dissection(jax.random.fold_in(seeds[6], 71), 0),
        "subtree_of": jax.random.permutation(seeds[2], SUBTREES).astype(jnp.int32),
        "fill_blocks": touch_ends((jax.random.randint(seeds[3], (SUBTREES * ROWBLOCKS, COLBLOCKS), 0, 2) < 1).astype(jnp.int32), jax.random.fold_in(seeds[3], 1), 0, 1),
        "leaf_shift": jnp.clip(jnp.exp(jax.random.uniform(seeds[4], (SUBTREES, FRONT), jnp.float32, math.log(0.5), math.log(4.0))), 0.5, 4.0),
        "separator_shift": jnp.clip(jnp.exp(math.log(4.0) - 2.0794415 * jax.random.uniform(seeds[5], (SSEP,), jnp.float32) ** level_of(seeds[5], (SSEP,), ((0, 4),), -0.2, 0.2)), 0.5, 4.0),
    }


def leaf_front(pix_cycle, cycle_to_dissection, fill_blocks, leaf_shift, subtree):
    rows = lax.dynamic_slice_in_dim(cycle_to_dissection, (subtree * ROWS).astype(jnp.int32), ROWS)
    design = pix_cycle[rows]
    pattern = lax.dynamic_slice_in_dim(fill_blocks, (subtree * ROWBLOCKS).astype(jnp.int32), ROWBLOCKS).astype(jnp.bfloat16)
    masked = (design.reshape(ROWBLOCKS, BLK, COLBLOCKS, BLK) * pattern[:, None, :, None]).reshape(ROWS, FRONT)
    front = jnp.dot(masked.T.astype(jnp.float32), masked.astype(jnp.float32), preferred_element_type=jnp.float32) / ROWS
    front = front + jnp.diag(leaf_shift[subtree])
    lower = jnp.linalg.cholesky(front[:KSUP, :KSUP])
    coupling = lax.linalg.triangular_solve(lower, front[KSUP:, :KSUP], left_side=False, lower=True, transpose_a=True)
    update = front[KSUP:, KSUP:] - jnp.dot(coupling, coupling.T, precision=lax.Precision.HIGHEST)
    return (lower, coupling, update)

def reference(pix_cycle, cycle_to_dissection, subtree_of, fill_blocks, leaf_shift, separator_shift):

    def advance(total, device):
        subtree = subtree_of[device]
        lower, coupling, update = leaf_front(pix_cycle, cycle_to_dissection, fill_blocks, leaf_shift, subtree)
        return (total + update, (lower, coupling))
    total, (lowers, couplings) = lax.scan(advance, jnp.zeros((SSEP, SSEP), jnp.float32), jnp.arange(N_LEAF, dtype=jnp.int32))
    separator = total / N_LEAF + jnp.diag(separator_shift)
    return (lowers.reshape(N_LEAF * KSUP, KSUP), couplings.reshape(N_LEAF * SSEP, KSUP), jnp.linalg.cholesky(separator))
```

```python
import jax
import jax.numpy as jnp
from jax import lax
from jax.experimental import pallas as pl
from jax.experimental.pallas import tpu as pltpu
from jax.sharding import PartitionSpec as P

KSUP = 512
SSEP = 1024
FRONT = KSUP + SSEP
BLK = 128
SLAB = 16
HIGHEST = lax.Precision.HIGHEST
VMEM_LIMIT = 60 << 20


def row_of(values, index):
    return jnp.broadcast_to(values[index : index + 1, :], (8, BLK))


def twice(values):
    return jnp.concatenate([values, values], 0)


def factor_block(block):
    lanes8 = lax.broadcasted_iota(jnp.int32, (8, BLK), 1)
    lanes = lax.broadcasted_iota(jnp.int32, (SLAB, BLK), 1)
    subs = lax.broadcasted_iota(jnp.int32, (SLAB, BLK), 0)
    count = BLK // SLAB
    work = [block[SLAB * s : SLAB * (s + 1), :] for s in range(count)]
    scaled = [None] * count
    corner = [None] * count
    for s in range(count):
        base = SLAB * s
        own = work[s]
        inside = (lanes >= base) & (lanes < base + SLAB)
        cols = []
        for j in range(SLAB):
            first = 8 if j >= 8 else 0
            cols.append(jnp.broadcast_to(own[first:, base + j : base + j + 1], (SLAB - first, BLK)))
        below = {
            b: [
                jnp.broadcast_to(work[b][:, base + j : base + j + 1], (SLAB, BLK))
                for j in range(SLAB)
            ]
            for b in range(s + 1, count)
        }
        start = jnp.where(inside, jnp.where(lanes - base == subs, 1.0, 0.0), own)
        rows = [row_of(start, j) for j in range(SLAB)]
        inv_pivot, scale, mult = [], [], {}
        for k in range(SLAB):
            off = 8 if k >= 8 else 0
            pivot = row_of(cols[k], k - off)
            inverse = 1.0 / pivot
            inv_pivot.append(inverse)
            scale.append(lax.rsqrt(pivot))
            for j in range(k + 1, SLAB):
                mult[k, j] = row_of(cols[k], j - off) * inverse
            for j in range(k + 1, SLAB):
                if j >= 8:
                    source = cols[k] if k >= 8 else cols[k][8:, :]
                    cols[j] = cols[j] - source * mult[k, j]
                else:
                    cols[j] = cols[j] - cols[k] * twice(mult[k, j])
                rows[j] = rows[j] - mult[k, j] * rows[k]
        solved = [rows[k] * inv_pivot[k] for k in range(SLAB)]
        for i in reversed(range(SLAB)):
            for k in range(i):
                solved[k] = solved[k] - mult[k, i] * solved[i]
        for b in range(s + 1, count):
            rest = jnp.where(inside, 0.0, work[b])
            for k in range(SLAB):
                rest = rest - below[b][k] * twice(solved[k])
            work[b] = rest
        out = jnp.zeros((SLAB, BLK), jnp.float32)
        low = jnp.zeros((SLAB, BLK), jnp.float32)
        for k in range(SLAB):
            out = jnp.where(subs == k, twice(rows[k] * scale[k]), out)
            if k >= 8:
                column = jnp.concatenate(
                    [jnp.zeros((8, BLK), jnp.float32), cols[k] * scale[k]], 0
                )
            else:
                column = cols[k] * twice(scale[k])
            low = jnp.where((lanes == base + k) & (subs >= k), column, low)
        scaled[s] = out
        corner[s] = low
    full = jnp.concatenate(scaled, 0)
    corners = jnp.concatenate(corner, 0)
    row_ids = lax.broadcasted_iota(jnp.int32, (BLK, BLK), 0)
    col_ids = lax.broadcasted_iota(jnp.int32, (BLK, BLK), 1)
    factor = jnp.where(row_ids // SLAB > col_ids // SLAB, full.T, corners)
    inverse = jnp.where(row_ids >= col_ids, full, 0.0)
    return factor, inverse


def dot_nt(a, b, precision=HIGHEST):
    return lax.dot_general(
        a, b, (((1,), (1,)), ((), ())), precision=precision, preferred_element_type=jnp.float32
    )


def dot_tn(a, b):
    return lax.dot_general(a, b, (((0,), (0,)), ((), ())), preferred_element_type=jnp.float32)


def eliminate(matrix, panel_ref, at, strips):
    rows = matrix.shape[0]
    factor, inverse = factor_block(matrix[pl.ds(at, BLK), pl.ds(at, BLK)])
    panel = dot_nt(matrix[:, pl.ds(at, BLK)], inverse)
    row_ids = lax.broadcasted_iota(jnp.int32, (rows, BLK), 0)
    panel = jnp.where(row_ids >= at + BLK, panel, 0.0)
    panel_ref[...] = panel
    matrix[:, pl.ds(at, BLK)] = panel
    matrix[pl.ds(at, BLK), pl.ds(at, BLK)] = factor
    for top, bottom, width in strips:

        @pl.when(width > at + BLK)
        def _():
            matrix[top:bottom, :width] = matrix[top:bottom, :width] - dot_nt(
                panel_ref[top:bottom, :], panel_ref[:width, :]
            )


def leaf_kernel(
    spot, design, position, pattern, shift, factor_out, coupling_out, blocks_out,
    masked, front, panel_ref, trail,
):
    panel_index = spot[0]
    rows = design.shape[1]
    piece = design.shape[2]
    here = lax.broadcasted_iota(jnp.int32, (rows, rows), 0)
    chosen = jnp.where(here == position[0:1, :], 1.0, 0.0).astype(jnp.bfloat16)
    fill = jnp.concatenate(
        [jnp.broadcast_to(pattern[b : b + 1, :], (BLK, BLK)) for b in range(rows // BLK)], 0
    )
    touch = jnp.dot(chosen, fill.astype(jnp.bfloat16), preferred_element_type=jnp.float32)
    for c in range(FRONT // BLK):
        p, at = c * BLK // piece, c * BLK % piece
        keep = jnp.broadcast_to(touch[:, c : c + 1], (rows, BLK)).astype(jnp.bfloat16)
        masked[:, c * BLK : (c + 1) * BLK] = design[p, :, at : at + BLK] * keep
    scale = 1.0 / rows
    for top in range(0, FRONT, 512):
        front[top : top + 512, :] = dot_tn(masked[:, top : top + 512], masked[:, :KSUP]) * scale
    row_ids = lax.broadcasted_iota(jnp.int32, (BLK, BLK), 0)
    col_ids = lax.broadcasted_iota(jnp.int32, (BLK, BLK), 1)
    same = row_ids == col_ids
    for b in range(KSUP // BLK):
        span = slice(b * BLK, (b + 1) * BLK)
        front[span, span] = front[span, span] + jnp.where(same, shift[0:1, span], 0.0)
    last = SSEP // BLK - 1
    halves = (panel_index, last - panel_index)
    for h, block_row in enumerate(halves):
        at = pl.multiple_of(KSUP + block_row * BLK, BLK)
        trail[h * BLK : (h + 1) * BLK, :] = (
            dot_tn(masked[:, pl.ds(at, BLK)], masked[:, KSUP:]) * scale
        )
        corner = pl.ds(pl.multiple_of(block_row * BLK, BLK), BLK)
        span = slice(h * BLK, (h + 1) * BLK)
        trail[span, corner] = trail[span, corner] + jnp.where(same, shift[0:1, pl.ds(at, BLK)], 0.0)

    strips = [(0, 256, 256), (256, FRONT, KSUP)]

    def step(j, carry):
        at = pl.multiple_of(j * BLK, BLK)
        eliminate(front, panel_ref, at, strips)

        @pl.when(j == panel_index)
        def _():
            factor_out[...] = front[:KSUP, pl.ds(at, BLK)]
            coupling_out[...] = front[KSUP:, pl.ds(at, BLK)]

        return carry

    lax.fori_loop(0, KSUP // BLK, step, 0)
    for h, block_row in enumerate(halves):
        at = pl.multiple_of(KSUP + block_row * BLK, BLK)
        span = slice(h * BLK, (h + 1) * BLK)
        trail[span, :] = trail[span, :] - dot_nt(front[pl.ds(at, BLK), :], front[KSUP:, :])

    def pack(i, carry):
        second = i > panel_index
        top = pl.multiple_of(jnp.where(second, BLK, 0), BLK)
        left = pl.multiple_of(jnp.where(second, i - panel_index - 1, i) * BLK, BLK)
        blocks_out[pl.ds(pl.multiple_of(i * BLK, BLK), BLK), :] = trail[
            pl.ds(top, BLK), pl.ds(left, BLK)
        ]
        return carry

    lax.fori_loop(0, last + 2, pack, 0)


def separator_kernel(spot, blocks, shift, out, matrix, panel_ref):
    size = SSEP // BLK
    share = 1.0 / 64
    row_ids = lax.broadcasted_iota(jnp.int32, (BLK, BLK), 0)
    col_ids = lax.broadcasted_iota(jnp.int32, (BLK, BLK), 1)
    for r in range(size):
        for c in range(size):
            span = (slice(r * BLK, (r + 1) * BLK), slice(c * BLK, (c + 1) * BLK))
            if c > r:
                matrix[span] = jnp.zeros((BLK, BLK), jnp.float32)
                continue
            p = min(r, size - 1 - r)
            i = c if r == p else p + 1 + c
            value = blocks[p, i * BLK : (i + 1) * BLK, :] * share
            if c == r:
                value = value + jnp.where(row_ids == col_ids, shift[0:1, span[1]], 0.0)
            matrix[span] = value
    strips = [(t, t + 256, t + 256) for t in range(0, SSEP, 256)]

    def step(j, carry):
        eliminate(matrix, panel_ref, pl.multiple_of(j * BLK, BLK), strips)
        return carry

    lax.fori_loop(0, size, step, 0)
    top = pl.multiple_of(spot[0] * out.shape[0], out.shape[0])
    left = pl.multiple_of(spot[1] * out.shape[1], out.shape[1])
    out[...] = matrix[pl.ds(top, out.shape[0]), pl.ds(left, out.shape[1])]


VM = pl.BlockSpec(memory_space=pltpu.VMEM)
SM = pl.BlockSpec(memory_space=pltpu.SMEM)


def per_device(
    pix_cycle, cycle_to_dissection, subtree_of, fill_blocks, leaf_shift, separator_shift
):
    leaves = lax.axis_size("leaf")
    panels = lax.axis_size("panel")
    rows, piece = pix_cycle.shape
    block_rows = rows // leaves
    leaf_index = lax.axis_index("leaf")
    panel_index = lax.axis_index("panel")
    subtree = subtree_of[leaf_index]
    outgoing = jnp.take(pix_cycle.reshape(leaves, block_rows, piece), subtree_of, axis=0)
    received = lax.all_to_all(
        outgoing.reshape(rows, piece), "leaf", split_axis=0, concat_axis=0, tiled=True
    )
    design = lax.all_gather(received, "panel", axis=0)
    cycle_index = lax.dynamic_slice_in_dim(cycle_to_dissection, subtree * rows, rows)
    position = (cycle_index // rows) * block_rows + cycle_index % rows - subtree * block_rows
    row_blocks = rows // BLK
    pattern = lax.dynamic_slice_in_dim(fill_blocks, subtree * row_blocks, row_blocks)
    pattern = jnp.pad(pattern, ((0, 0), (0, BLK - pattern.shape[1]))).astype(jnp.float32)
    shift = lax.dynamic_slice_in_dim(leaf_shift, subtree, 1, 0)
    count = SSEP // BLK + 1
    factor_cols, coupling_cols, blocks = pl.pallas_call(
        leaf_kernel,
        out_shape=(
            jax.ShapeDtypeStruct((KSUP, KSUP // panels), jnp.float32),
            jax.ShapeDtypeStruct((SSEP, KSUP // panels), jnp.float32),
            jax.ShapeDtypeStruct((count * BLK, BLK), jnp.float32),
        ),
        in_specs=[SM, VM, VM, VM, VM],
        out_specs=(VM, VM, VM),
        scratch_shapes=[
            pltpu.VMEM((rows, FRONT), jnp.bfloat16),
            pltpu.VMEM((FRONT, KSUP), jnp.float32),
            pltpu.VMEM((FRONT, BLK), jnp.float32),
            pltpu.VMEM((2 * BLK, SSEP), jnp.float32),
        ],
        compiler_params=pltpu.CompilerParams(vmem_limit_bytes=VMEM_LIMIT),
        name="leaf_front",
    )(panel_index[None], design, position[None], pattern, shift)
    summed = lax.psum(blocks, "leaf")
    whole = lax.all_gather(summed, "panel", axis=0)
    shifts = lax.all_gather(separator_shift, "panel", axis=0, tiled=True)
    result_rows = pl.pallas_call(
        separator_kernel,
        out_shape=jax.ShapeDtypeStruct((SSEP // leaves, SSEP // panels), jnp.float32),
        in_specs=[SM, VM, VM],
        out_specs=VM,
        scratch_shapes=[
            pltpu.VMEM((SSEP, SSEP), jnp.float32),
            pltpu.VMEM((SSEP, BLK), jnp.float32),
        ],
        compiler_params=pltpu.CompilerParams(vmem_limit_bytes=VMEM_LIMIT),
        name="separator_front",
    )(jnp.stack([leaf_index, panel_index]), whole, shifts[None])
    return (factor_cols, coupling_cols, result_rows)


def solution(mesh):
    placed = (P("leaf", "panel"), P(), P(), P(), P(), P("panel"))
    return jax.shard_map(
        per_device,
        mesh=mesh,
        in_specs=placed,
        out_specs=(P("leaf", "panel"), P("leaf", "panel"), P("leaf", "panel")),
        check_vma=False,
    )
```

```python
import jax
import jax.numpy as jnp
from jax import lax
from jax.experimental import pallas as pl
from jax.experimental.pallas import tpu as pltpu
from jax.sharding import PartitionSpec as P

KSUP = 512
SSEP = 1024
FRONT = KSUP + SSEP
BLK = 128
SLAB = 16
HIGHEST = lax.Precision.HIGHEST
VMEM_LIMIT = 60 << 20


def row_of(values, index):
    return jnp.broadcast_to(values[index : index + 1, :], (8, BLK))


def twice(values):
    return jnp.concatenate([values, values], 0)


def factor_block(block):
    lanes8 = lax.broadcasted_iota(jnp.int32, (8, BLK), 1)
    lanes = lax.broadcasted_iota(jnp.int32, (SLAB, BLK), 1)
    subs = lax.broadcasted_iota(jnp.int32, (SLAB, BLK), 0)
    count = BLK // SLAB
    work = [block[SLAB * s : SLAB * (s + 1), :] for s in range(count)]
    scaled = [None] * count
    corner = [None] * count
    for s in range(count):
        base = SLAB * s
        own = work[s]
        inside = (lanes >= base) & (lanes < base + SLAB)
        cols = []
        for j in range(SLAB):
            first = 8 if j >= 8 else 0
            cols.append(jnp.broadcast_to(own[first:, base + j : base + j + 1], (SLAB - first, BLK)))
        below = {
            b: [
                jnp.broadcast_to(work[b][:, base + j : base + j + 1], (SLAB, BLK))
                for j in range(SLAB)
            ]
            for b in range(s + 1, count)
        }
        start = jnp.where(inside, jnp.where(lanes - base == subs, 1.0, 0.0), own)
        rows = [row_of(start, j) for j in range(SLAB)]
        inv_pivot, scale, mult = [], [], {}
        for k in range(SLAB):
            off = 8 if k >= 8 else 0
            pivot = row_of(cols[k], k - off)
            inverse = 1.0 / pivot
            inv_pivot.append(inverse)
            scale.append(lax.rsqrt(pivot))
            for j in range(k + 1, SLAB):
                mult[k, j] = row_of(cols[k], j - off) * inverse
            for j in range(k + 1, SLAB):
                if j >= 8:
                    source = cols[k] if k >= 8 else cols[k][8:, :]
                    cols[j] = cols[j] - source * mult[k, j]
                else:
                    cols[j] = cols[j] - cols[k] * twice(mult[k, j])
                rows[j] = rows[j] - mult[k, j] * rows[k]
        solved = [rows[k] * inv_pivot[k] for k in range(SLAB)]
        for i in reversed(range(SLAB)):
            for k in range(i):
                solved[k] = solved[k] - mult[k, i] * solved[i]
        for b in range(s + 1, count):
            rest = jnp.where(inside, 0.0, work[b])
            for k in range(SLAB):
                rest = rest - below[b][k] * twice(solved[k])
            work[b] = rest
        out = jnp.zeros((SLAB, BLK), jnp.float32)
        low = jnp.zeros((SLAB, BLK), jnp.float32)
        for k in range(SLAB):
            out = jnp.where(subs == k, twice(rows[k] * scale[k]), out)
            if k >= 8:
                column = jnp.concatenate(
                    [jnp.zeros((8, BLK), jnp.float32), cols[k] * scale[k]], 0
                )
            else:
                column = cols[k] * twice(scale[k])
            low = jnp.where((lanes == base + k) & (subs >= k), column, low)
        scaled[s] = out
        corner[s] = low
    full = jnp.concatenate(scaled, 0)
    corners = jnp.concatenate(corner, 0)
    row_ids = lax.broadcasted_iota(jnp.int32, (BLK, BLK), 0)
    col_ids = lax.broadcasted_iota(jnp.int32, (BLK, BLK), 1)
    factor = jnp.where(row_ids // SLAB > col_ids // SLAB, full.T, corners)
    inverse = jnp.where(row_ids >= col_ids, full, 0.0)
    return factor, inverse


def dot_nt(a, b, precision=HIGHEST):
    return lax.dot_general(
        a, b, (((1,), (1,)), ((), ())), precision=precision, preferred_element_type=jnp.float32
    )


def dot_tn(a, b):
    return lax.dot_general(a, b, (((0,), (0,)), ((), ())), preferred_element_type=jnp.float32)


def eliminate(matrix, panel_ref, at, strips):
    rows = matrix.shape[0]
    factor, inverse = factor_block(matrix[pl.ds(at, BLK), pl.ds(at, BLK)])
    panel = dot_nt(matrix[:, pl.ds(at, BLK)], inverse)
    row_ids = lax.broadcasted_iota(jnp.int32, (rows, BLK), 0)
    panel = jnp.where(row_ids >= at + BLK, panel, 0.0)
    panel_ref[...] = panel
    matrix[:, pl.ds(at, BLK)] = panel
    matrix[pl.ds(at, BLK), pl.ds(at, BLK)] = factor
    for top, bottom, width in strips:

        @pl.when(width > at + BLK)
        def _():
            matrix[top:bottom, :width] = matrix[top:bottom, :width] - dot_nt(
                panel_ref[top:bottom, :], panel_ref[:width, :]
            )


def leaf_kernel(
    spot, design, position, pattern, shift, factor_out, coupling_out, blocks_out,
    masked, front, panel_ref, trail,
):
    panel_index = spot[0]
    rows = design.shape[1]
    piece = design.shape[2]
    here = lax.broadcasted_iota(jnp.int32, (rows, rows), 0)
    chosen = jnp.where(here == position[0:1, :], 1.0, 0.0).astype(jnp.bfloat16)
    fill = jnp.concatenate(
        [jnp.broadcast_to(pattern[b : b + 1, :], (BLK, BLK)) for b in range(rows // BLK)], 0
    )
    touch = jnp.dot(chosen, fill.astype(jnp.bfloat16), preferred_element_type=jnp.float32)
    for c in range(FRONT // BLK):
        p, at = c * BLK // piece, c * BLK % piece
        keep = jnp.broadcast_to(touch[:, c : c + 1], (rows, BLK)).astype(jnp.bfloat16)
        masked[:, c * BLK : (c + 1) * BLK] = design[p, :, at : at + BLK] * keep
    scale = 1.0 / rows
    for top in range(0, FRONT, 512):
        front[top : top + 512, :] = dot_tn(masked[:, top : top + 512], masked[:, :KSUP]) * scale
    row_ids = lax.broadcasted_iota(jnp.int32, (BLK, BLK), 0)
    col_ids = lax.broadcasted_iota(jnp.int32, (BLK, BLK), 1)
    same = row_ids == col_ids
    for b in range(KSUP // BLK):
        span = slice(b * BLK, (b + 1) * BLK)
        front[span, span] = front[span, span] + jnp.where(same, shift[0:1, span], 0.0)
    last = SSEP // BLK - 1
    halves = (panel_index, last - panel_index)
    for h, block_row in enumerate(halves):
        at = pl.multiple_of(KSUP + block_row * BLK, BLK)
        trail[h * BLK : (h + 1) * BLK, :] = (
            dot_tn(masked[:, pl.ds(at, BLK)], masked[:, KSUP:]) * scale
        )
        corner = pl.ds(pl.multiple_of(block_row * BLK, BLK), BLK)
        span = slice(h * BLK, (h + 1) * BLK)
        trail[span, corner] = trail[span, corner] + jnp.where(same, shift[0:1, pl.ds(at, BLK)], 0.0)

    strips = [(0, 256, 256), (256, FRONT, KSUP)]

    def step(j, carry):
        at = pl.multiple_of(j * BLK, BLK)
        eliminate(front, panel_ref, at, strips)

        @pl.when(j == panel_index)
        def _():
            factor_out[...] = front[:KSUP, pl.ds(at, BLK)]
            coupling_out[...] = front[KSUP:, pl.ds(at, BLK)]

        return carry

    lax.fori_loop(0, KSUP // BLK, step, 0)
    for h, block_row in enumerate(halves):
        at = pl.multiple_of(KSUP + block_row * BLK, BLK)
        span = slice(h * BLK, (h + 1) * BLK)
        trail[span, :] = trail[span, :] - dot_nt(front[pl.ds(at, BLK), :], front[KSUP:, :])

    def pack(i, carry):
        second = i > panel_index
        top = pl.multiple_of(jnp.where(second, BLK, 0), BLK)
        left = pl.multiple_of(jnp.where(second, i - panel_index - 1, i) * BLK, BLK)
        blocks_out[pl.ds(pl.multiple_of(i * BLK, BLK), BLK), :] = trail[
            pl.ds(top, BLK), pl.ds(left, BLK)
        ]
        return carry

    lax.fori_loop(0, last + 2, pack, 0)


def separator_kernel(spot, blocks, shift, out, matrix, panel_ref):
    size = SSEP // BLK
    share = 1.0 / 64
    row_ids = lax.broadcasted_iota(jnp.int32, (BLK, BLK), 0)
    col_ids = lax.broadcasted_iota(jnp.int32, (BLK, BLK), 1)
    for r in range(size):
        for c in range(size):
            span = (slice(r * BLK, (r + 1) * BLK), slice(c * BLK, (c + 1) * BLK))
            if c > r:
                matrix[span] = jnp.zeros((BLK, BLK), jnp.float32)
                continue
            p = min(r, size - 1 - r)
            i = c if r == p else p + 1 + c
            value = blocks[p, i * BLK : (i + 1) * BLK, :] * share
            if c == r:
                value = value + jnp.where(row_ids == col_ids, shift[r // 2, r % 2 : r % 2 + 1, :], 0.0)
            matrix[span] = value
    strips = [(t, t + 256, t + 256) for t in range(0, SSEP, 256)]

    def step(j, carry):
        eliminate(matrix, panel_ref, pl.multiple_of(j * BLK, BLK), strips)
        return carry

    lax.fori_loop(0, size, step, 0)
    top = pl.multiple_of(spot[0] * out.shape[0], out.shape[0])
    left = pl.multiple_of(spot[1] * out.shape[1], out.shape[1])
    out[...] = matrix[pl.ds(top, out.shape[0]), pl.ds(left, out.shape[1])]


VM = pl.BlockSpec(memory_space=pltpu.VMEM)
SM = pl.BlockSpec(memory_space=pltpu.SMEM)
MESH = pl.DeviceIdType.MESH
Z, X, Y, LO = 8, 4, 4, 2


def place():
    leaf = lax.axis_index("leaf")
    panel = lax.axis_index("panel")
    z = leaf // (X * LO)
    x = leaf // LO % X
    y = panel // 2 * LO + leaf % LO
    return z, x, y, panel % 2


def device_at(z, x, y, core):
    return ((z * X + x) * LO + y % LO, y // LO * 2 + core)


def copy_to(source, target, sent, landed, device):
    return pltpu.make_async_remote_copy(
        src_ref=source, dst_ref=target, send_sem=sent, recv_sem=landed, device_id=device, device_id_type=MESH
    )


def greet(devices):
    barrier = pltpu.get_barrier_semaphore()
    for device in devices:
        pl.semaphore_signal(barrier, inc=1, device_id=device, device_id_type=MESH)
    pl.semaphore_wait(barrier, len(devices))


TILES = 18
STARTS = [15 * i // 7 for i in range(Z)]


def sum_kernel(
    blocks, shift, whole, shifts,
    landed_a, partial, landed_b, reduced, gathered,
    sent_a, got_a, sent_b, got_b, sent_c, got_c, local,
    sent_1, got_1, sent_2, got_2, sent_s, got_s, sent_h, got_h,
):
    z, x, y, core = place()
    lo, hi = y % LO, y // LO
    piece = TILES * 8
    half = piece // 2
    plane = [(dx, dy) for dx in range(X) for dy in range(LO) if dx or dy]

    def at_plane(dx, dy):
        return device_at(z, (x + dx) % X, hi * LO + (lo + dy) % LO, core)

    def at_z(d):
        return device_at((z + d) % Z, x, y, core)

    def at_y(d):
        return device_at(z, x, (y + d) % Y, core)

    def at_x(d):
        return device_at(z, (x + d) % X, y, core)

    sibling = device_at(z, x, y, 1 - core)
    greet(
        [at_plane(*d) for d in plane]
        + [at_z(d) for d in range(1, Z)]
        + [at_y(d) for d in range(1, Y)]
        + [sibling]
    )
    pending = []

    def go(copy):
        copy.start()
        pending.append(copy)
        return copy

    def rows_of(x_at, y_at):
        return pl.multiple_of((x_at * LO + y_at % LO) * piece, 8)

    def panel_of(y_at, core_at):
        return y_at // LO * 2 + core_at

    own_panel = panel_of(y, core)
    go(copy_to(shift, shifts.at[own_panel], sent_h.at[0], got_h.at[0], at_y(2)))
    go(copy_to(shift, shifts.at[own_panel], sent_h.at[1], got_h.at[1], sibling))
    keep = pltpu.make_async_copy(shift, shifts.at[own_panel], local.at[Z])
    keep.start()

    first = []
    for dx, dy in plane:
        i = dx * LO + dy
        at = rows_of((x + dx) % X, lo + dy)
        first.append(
            go(copy_to(blocks.at[pl.ds(at, piece), :], landed_a.at[i], sent_a.at[i], got_a.at[i], at_plane(dx, dy)))
        )
    total = blocks[pl.ds(rows_of(x, lo), piece), :]
    for (dx, dy), copy in zip(plane, first):
        copy.wait_recv()
        total = total + landed_a[dx * LO + dy]
    partial[...] = total

    def start_of(z_at):
        return pl.multiple_of(15 * z_at // 7 * 8, 8)

    second = []
    for d in range(1, Z):
        source = partial.at[pl.ds(start_of((z + d) % Z), 24), :]
        second.append(go(copy_to(source, landed_b.at[d], sent_b.at[d], got_b.at[d], at_z(d))))
    total = partial[pl.ds(start_of(z), 24), :]
    for d, copy in zip(range(1, Z), second):
        copy.wait_recv()
        total = total + landed_b[d]
    reduced[...] = total

    third = [
        go(copy_to(reduced, gathered.at[z], sent_c.at[d], got_c.at[d], at_z(d))) for d in range(1, Z)
    ]
    mine = pltpu.make_async_copy(reduced, gathered.at[z], local.at[0])
    mine.start()
    pending[0].wait_recv()
    go(copy_to(shifts.at[panel_of(y + 2 - y // 2 * 4, core)], shifts.at[panel_of(y + 2 - y // 2 * 4, core)],
               sent_h.at[2], got_h.at[2], sibling))
    mine.wait()
    for copy in third:
        copy.wait_recv()
    top = rows_of(x, y)
    own = whole.at[own_panel, pl.ds(top, piece), :]
    moves = []
    for i in range(Z):
        length = ((STARTS + [TILES])[i + 1] - STARTS[i]) * 8
        move = pltpu.make_async_copy(
            gathered.at[i, 0:length, :],
            whole.at[own_panel, pl.ds(pl.multiple_of(top + STARTS[i] * 8, 8), length), :],
            local.at[i],
        )
        move.start()
        moves.append(move)
    for move in moves:
        move.wait()

    def part(x_at, y_at, side, core_at=core):
        at = pl.multiple_of(rows_of(x_at, y_at) + side * half, 8)
        return whole.at[panel_of(y_at, core_at), pl.ds(at, half), :]

    def pass_on(ref, sems_sent, sems_got, index, device):
        return go(copy_to(ref, ref, sems_sent.at[index], sems_got.at[index], device))

    ring = [at_y, at_x]
    length = Y
    first_wave = {}
    for side in range(2):
        for d in range(1, length):
            first_wave[side, d] = pass_on(part(x, y, side), sent_1, got_1, side * 4 + d, ring[side](d))
    second_wave = []

    def spread(side, d):
        where = part(x, (y - d) % Y, 0) if side == 0 else part((x - d) % X, y, 1)
        for e in range(1, length):
            second_wave.append(
                (side, d, e, pass_on(where, sent_2, got_2, (side * 4 + d) * 4 + e, ring[1 - side](e)))
            )
        pass_on(where, sent_s, got_s, (side * 4 + d) * 4, sibling)

    for side in range(2):
        spread(side, 0)
    for d in range(1, length):
        for side in range(2):
            first_wave[side, d].wait_recv()
            spread(side, d)
    for side, d, e, copy in second_wave:
        copy.wait_recv()
        if side == 0:
            where = part((x - e) % X, (y - d) % Y, 0)
        else:
            where = part((x - d) % X, (y - e) % Y, 1)
        pass_on(where, sent_s, got_s, (side * 4 + d) * 4 + e, sibling)
    for copy in pending:
        copy.wait_send()
    for side in range(2):
        for d in range(length):
            for e in range(length):
                if side == 0:
                    where = part((x - e) % X, (y - d) % Y, 0, 1 - core)
                else:
                    where = part((x - d) % X, (y - e) % Y, 1, 1 - core)
                index = (side * 4 + d) * 4 + e
                copy_to(where, where, sent_s.at[index], got_s.at[index], sibling).wait_recv()
    keep.wait()
    for i, panel in ((1, panel_of(y, 1 - core)), (2, panel_of(y + 2 - y // 2 * 4, 1 - core))):
        copy_to(shift, shifts.at[panel], sent_h.at[i], got_h.at[i], sibling).wait_recv()


def sum_blocks(blocks, shift):
    rows = blocks.shape[0]
    dma = pltpu.SemaphoreType.DMA
    f32 = jnp.float32
    return pl.pallas_call(
        sum_kernel,
        out_shape=(
            jax.ShapeDtypeStruct((4, rows, BLK), f32),
            jax.ShapeDtypeStruct((4, 2, BLK), f32),
        ),
        in_specs=[VM, VM],
        out_specs=(VM, VM),
        scratch_shapes=[
            pltpu.VMEM((8, TILES * 8, BLK), f32),
            pltpu.VMEM((TILES * 8, BLK), f32),
            pltpu.VMEM((Z, 24, BLK), f32),
            pltpu.VMEM((24, BLK), f32),
            pltpu.VMEM((Z, 24, BLK), f32),
            dma((8,)), dma((8,)), dma((8,)), dma((8,)), dma((8,)), dma((8,)), dma((Z + 1,)),
            dma((8,)), dma((8,)), dma((32,)), dma((32,)), dma((32,)), dma((32,)), dma((3,)), dma((3,)),
        ],
        compiler_params=pltpu.CompilerParams(collective_id=1, has_side_effects=True, vmem_limit_bytes=40 << 20),
        name="separator_sum",
    )(blocks, shift)


ORDER = (0, 1, 7, 2, 6, 3, 5, 4)


def relay(along, dz, slab, go, sent_s, got_s, sibling):
    for d in (1, 3, 2):
        along[dz, d].wait_recv()
        i = dz * Y + d
        go(copy_to(slab(dz, d), slab(dz, d), sent_s.at[i], got_s.at[i], sibling))


def exchange_kernel(outgoing, design, middle, local, sent_a, got_a, sent_y, got_y, sent_s, got_s):
    z, x, y, core = place()
    own_panel = y // LO * 2 + core
    sibling = device_at(z, x, y, 1 - core)
    near = [(dz, dx) for dz in ORDER for dx in range(X) if dz or dx]

    def at(dz, dx):
        return device_at((z + dz) % Z, (x + dx) % X, y, core)

    def at_y(d):
        return device_at(z, x, (y + d) % Y, core)

    greet([at(*d) for d in near] + [at_y(d) for d in range(1, Y)] + [sibling])
    pending = []

    def go(copy):
        copy.start()
        pending.append(copy)
        return copy

    arrive = {}
    keep = pltpu.make_async_copy(outgoing.at[z, x], middle.at[z, x], local.at[Z])
    keep.start()
    for dz, dx in near:
        i = dz * X + dx
        arrive[dz, dx] = go(
            copy_to(
                outgoing.at[(z + dz) % Z, (x + dx) % X], middle.at[z, x], sent_a.at[i], got_a.at[i], at(dz, dx)
            )
        )
    along = {}
    moves = []

    def slab(dz, d):
        y_from = (y - d) % Y
        return design.at[y_from // LO * 2 + core, (z - dz) % Z, :, y_from % LO]

    for n, dz in enumerate(ORDER):
        for dx in range(X):
            if dz or dx:
                arrive[dz, dx].wait_recv()
        if dz == 0:
            keep.wait()
        z_from = (z - dz) % Z
        target = design.at[own_panel, z_from, :, y % LO]
        other = middle.at[z_from, :, 1 - y % LO]
        same = middle.at[z_from, :, y % LO]
        for d in (2, 1, 3):
            source = same if d == 2 else other
            i = dz * Y + d
            along[dz, d] = go(copy_to(source, target, sent_y.at[i], got_y.at[i], at_y(d)))
        go(copy_to(same, target, sent_s.at[dz * Y], got_s.at[dz * Y], sibling))
        move = pltpu.make_async_copy(same, target, local.at[dz])
        move.start()
        moves.append(move)
        if n:
            relay(along, ORDER[n - 1], slab, go, sent_s, got_s, sibling)
    relay(along, ORDER[-1], slab, go, sent_s, got_s, sibling)
    for copy in pending:
        copy.wait_send()
    for move in moves:
        move.wait()
    for dz in ORDER:
        for d in range(Y):
            i = dz * Y + d
            copy_to(slab(dz, d), slab(dz, d), sent_s.at[i], got_s.at[i], sibling).wait_recv()


def exchange(outgoing):
    dma = pltpu.SemaphoreType.DMA
    rows, piece = outgoing.shape[-2:]
    return pl.pallas_call(
        exchange_kernel,
        out_shape=jax.ShapeDtypeStruct((4,) + outgoing.shape, outgoing.dtype),
        in_specs=[VM],
        out_specs=VM,
        scratch_shapes=[pltpu.VMEM(outgoing.shape, outgoing.dtype), dma((Z + 1,))]
        + [dma((Z * X,)) for _ in range(6)],
        compiler_params=pltpu.CompilerParams(collective_id=2, has_side_effects=True, vmem_limit_bytes=40 << 20),
        name="design_exchange",
    )(outgoing)


def per_device(
    pix_cycle, cycle_to_dissection, subtree_of, fill_blocks, leaf_shift, separator_shift
):
    leaves = lax.axis_size("leaf")
    panels = lax.axis_size("panel")
    rows, piece = pix_cycle.shape
    block_rows = rows // leaves
    leaf_index = lax.axis_index("leaf")
    panel_index = lax.axis_index("panel")
    subtree = subtree_of[leaf_index]
    outgoing = jnp.take(pix_cycle.reshape(leaves, block_rows, piece), subtree_of, axis=0)
    received = exchange(outgoing.reshape(Z, X, LO, block_rows, piece))
    design = received.reshape(panels, rows, piece)
    cycle_index = lax.dynamic_slice_in_dim(cycle_to_dissection, subtree * rows, rows)
    position = (cycle_index // rows) * block_rows + cycle_index % rows - subtree * block_rows
    row_blocks = rows // BLK
    pattern = lax.dynamic_slice_in_dim(fill_blocks, subtree * row_blocks, row_blocks)
    pattern = jnp.pad(pattern, ((0, 0), (0, BLK - pattern.shape[1]))).astype(jnp.float32)
    shift = lax.dynamic_slice_in_dim(leaf_shift, subtree, 1, 0)
    count = SSEP // BLK + 1
    factor_cols, coupling_cols, blocks = pl.pallas_call(
        leaf_kernel,
        out_shape=(
            jax.ShapeDtypeStruct((KSUP, KSUP // panels), jnp.float32),
            jax.ShapeDtypeStruct((SSEP, KSUP // panels), jnp.float32),
            jax.ShapeDtypeStruct((count * BLK, BLK), jnp.float32),
        ),
        in_specs=[SM, VM, VM, VM, VM],
        out_specs=(VM, VM, VM),
        scratch_shapes=[
            pltpu.VMEM((rows, FRONT), jnp.bfloat16),
            pltpu.VMEM((FRONT, KSUP), jnp.float32),
            pltpu.VMEM((FRONT, BLK), jnp.float32),
            pltpu.VMEM((2 * BLK, SSEP), jnp.float32),
        ],
        compiler_params=pltpu.CompilerParams(vmem_limit_bytes=VMEM_LIMIT),
        name="leaf_front",
    )(panel_index[None], design, position[None], pattern, shift)
    whole, shifts = sum_blocks(blocks, separator_shift.reshape(2, BLK))
    result_rows = pl.pallas_call(
        separator_kernel,
        out_shape=jax.ShapeDtypeStruct((SSEP // leaves, SSEP // panels), jnp.float32),
        in_specs=[SM, VM, VM],
        out_specs=VM,
        scratch_shapes=[
            pltpu.VMEM((SSEP, SSEP), jnp.float32),
            pltpu.VMEM((SSEP, BLK), jnp.float32),
        ],
        compiler_params=pltpu.CompilerParams(vmem_limit_bytes=VMEM_LIMIT),
        name="separator_front",
    )(jnp.stack([leaf_index, panel_index]), whole, shifts)
    return (factor_cols, coupling_cols, result_rows)


def solution(mesh):
    placed = (P("leaf", "panel"), P(), P(), P(), P(), P("panel"))
    return jax.shard_map(
        per_device,
        mesh=mesh,
        in_specs=placed,
        out_specs=(P("leaf", "panel"), P("leaf", "panel"), P("leaf", "panel")),
        check_vma=False,
    )
```

```python
import jax
import jax.numpy as jnp
from jax import lax
from jax.experimental import pallas as pl
from jax.experimental.pallas import tpu as pltpu
from jax.sharding import PartitionSpec as P

KSUP = 512
SSEP = 1024
FRONT = KSUP + SSEP
BLK = 128
SLAB = 16
HIGHEST = lax.Precision.HIGHEST
VMEM_LIMIT = 60 << 20


def row_of(values, index):
    return jnp.broadcast_to(values[index : index + 1, :], (8, BLK))


def twice(values):
    return jnp.concatenate([values, values], 0)


def factor_block(block):
    lanes8 = lax.broadcasted_iota(jnp.int32, (8, BLK), 1)
    lanes = lax.broadcasted_iota(jnp.int32, (SLAB, BLK), 1)
    subs = lax.broadcasted_iota(jnp.int32, (SLAB, BLK), 0)
    count = BLK // SLAB
    work = [block[SLAB * s : SLAB * (s + 1), :] for s in range(count)]
    scaled = [None] * count
    corner = [None] * count
    for s in range(count):
        base = SLAB * s
        own = work[s]
        inside = (lanes >= base) & (lanes < base + SLAB)
        cols = []
        for j in range(SLAB):
            first = 8 if j >= 8 else 0
            cols.append(jnp.broadcast_to(own[first:, base + j : base + j + 1], (SLAB - first, BLK)))
        below = {
            b: [
                jnp.broadcast_to(work[b][:, base + j : base + j + 1], (SLAB, BLK))
                for j in range(SLAB)
            ]
            for b in range(s + 1, count)
        }
        start = jnp.where(inside, jnp.where(lanes - base == subs, 1.0, 0.0), own)
        rows = [row_of(start, j) for j in range(SLAB)]
        inv_pivot, scale, mult = [], [], {}
        for k in range(SLAB):
            off = 8 if k >= 8 else 0
            pivot = row_of(cols[k], k - off)
            inverse = 1.0 / pivot
            inv_pivot.append(inverse)
            scale.append(lax.rsqrt(pivot))
            for j in range(k + 1, SLAB):
                mult[k, j] = row_of(cols[k], j - off) * inverse
            for j in range(k + 1, SLAB):
                if j >= 8:
                    source = cols[k] if k >= 8 else cols[k][8:, :]
                    cols[j] = cols[j] - source * mult[k, j]
                else:
                    cols[j] = cols[j] - cols[k] * twice(mult[k, j])
                rows[j] = rows[j] - mult[k, j] * rows[k]
        solved = [rows[k] * inv_pivot[k] for k in range(SLAB)]
        for i in reversed(range(SLAB)):
            for k in range(i):
                solved[k] = solved[k] - mult[k, i] * solved[i]
        for b in range(s + 1, count):
            rest = jnp.where(inside, 0.0, work[b])
            for k in reversed(range(SLAB)):
                rest = rest - below[b][k] * twice(solved[k])
            work[b] = rest
        out = jnp.zeros((SLAB, BLK), jnp.float32)
        low = jnp.zeros((SLAB, BLK), jnp.float32)
        for k in range(SLAB):
            out = jnp.where(subs == k, twice(rows[k] * scale[k]), out)
            if k >= 8:
                column = jnp.concatenate(
                    [jnp.zeros((8, BLK), jnp.float32), cols[k] * scale[k]], 0
                )
            else:
                column = cols[k] * twice(scale[k])
            low = jnp.where((lanes == base + k) & (subs >= k), column, low)
        scaled[s] = out
        corner[s] = low
    full = jnp.concatenate(scaled, 0)
    corners = jnp.concatenate(corner, 0)
    row_ids = lax.broadcasted_iota(jnp.int32, (BLK, BLK), 0)
    col_ids = lax.broadcasted_iota(jnp.int32, (BLK, BLK), 1)
    factor = jnp.where(row_ids // SLAB > col_ids // SLAB, full.T, corners)
    inverse = jnp.where(row_ids >= col_ids, full, 0.0)
    return factor, inverse


def dot_nt(a, b, precision=HIGHEST):
    return lax.dot_general(
        a, b, (((1,), (1,)), ((), ())), precision=precision, preferred_element_type=jnp.float32
    )


def dot_tn(a, b):
    return lax.dot_general(a, b, (((0,), (0,)), ((), ())), preferred_element_type=jnp.float32)


def split_parts(values):
    high = values.astype(jnp.bfloat16)
    rest = values - high.astype(jnp.float32)
    middle = rest.astype(jnp.bfloat16)
    low = (rest - middle.astype(jnp.float32)).astype(jnp.bfloat16)
    left = jnp.concatenate([high, middle, high, middle, high, low], 1)
    right = jnp.concatenate([high, high, middle, middle, low, high], 1)
    return left, right


def make_panel(matrix, inverse, factor, left, right, at):
    rows = matrix.shape[0]
    panel = dot_nt(matrix[:, pl.ds(at, BLK)], inverse)
    row_ids = lax.broadcasted_iota(jnp.int32, (rows, BLK), 0)
    panel = jnp.where(row_ids >= at + BLK, panel, 0.0)
    left[...], right[...] = split_parts(panel)
    matrix[:, pl.ds(at, BLK)] = panel
    matrix[pl.ds(at, BLK), pl.ds(at, BLK)] = factor


def next_block(matrix, inverse, at):
    after = pl.multiple_of(at + BLK, BLK)
    head = dot_nt(matrix[pl.ds(after, BLK), pl.ds(at, BLK)], inverse)
    return matrix[pl.ds(after, BLK), pl.ds(after, BLK)] - dot_nt(head, head)


def subtract(matrix, left, right, strips):
    for top, bottom, width in strips:
        matrix[top:bottom, :width] = matrix[top:bottom, :width] - dot_nt(
            left[top:bottom, :], right[:width, :], None
        )


def leaf_kernel(
    spot, design, touch, shift_rows, factor_out, coupling_out, blocks_out,
    masked, front, left, right, trail, inverse_ref, factor_ref, shift,
):
    panel_index = spot[0]
    rows = design.shape[1]
    piece = design.shape[2]
    shift[...] = shift_rows[pl.ds(spot[1], 1), :]
    for c in range(FRONT // BLK):
        p, at = c * BLK // piece, c * BLK % piece
        keep = jnp.broadcast_to(touch[:, c : c + 1], (rows, BLK)).astype(jnp.bfloat16)
        masked[:, c * BLK : (c + 1) * BLK] = design[p, :, at : at + BLK] * keep
    scale = 1.0 / rows
    for top in range(0, FRONT, 512):
        front[top : top + 512, :] = dot_tn(masked[:, top : top + 512], masked[:, :KSUP]) * scale
    row_ids = lax.broadcasted_iota(jnp.int32, (BLK, BLK), 0)
    col_ids = lax.broadcasted_iota(jnp.int32, (BLK, BLK), 1)
    same = row_ids == col_ids
    for b in range(KSUP // BLK):
        span = slice(b * BLK, (b + 1) * BLK)
        front[span, span] = front[span, span] + jnp.where(same, shift[:, span], 0.0)
    last = SSEP // BLK - 1
    halves = (panel_index, last - panel_index)
    for h, block_row in enumerate(halves):
        at = pl.multiple_of(KSUP + block_row * BLK, BLK)
        trail[h * BLK : (h + 1) * BLK, :] = (
            dot_tn(masked[:, pl.ds(at, BLK)], masked[:, KSUP:]) * scale
        )
        corner = pl.ds(pl.multiple_of(block_row * BLK, BLK), BLK)
        span = slice(h * BLK, (h + 1) * BLK)
        line = shift[:, pl.ds(at, BLK)]
        trail[span, corner] = trail[span, corner] + jnp.where(same, line, 0.0)

    def subtract_trail():
        for h, block_row in enumerate(halves):
            at = pl.multiple_of(KSUP + block_row * BLK, BLK)
            span = slice(h * BLK, (h + 1) * BLK)
            trail[span, :] = trail[span, :] - dot_nt(left[pl.ds(at, BLK), :], right[KSUP:, :], None)

    factor_ref[...], inverse_ref[...] = factor_block(front[:BLK, :BLK])

    def step(j, carry):
        at = pl.multiple_of(j * BLK, BLK)
        inverse = inverse_ref[...]
        block = next_block(front, inverse, at)
        make_panel(front, inverse, factor_ref[...], left, right, at)
        subtract(front, left, right, [(BLK, 256, 256), (256, FRONT, KSUP)])
        subtract_trail()
        factor_ref[...], inverse_ref[...] = factor_block(block)
        return carry

    lax.fori_loop(0, KSUP // BLK - 1, step, 0)
    make_panel(front, inverse_ref[...], factor_ref[...], left, right, KSUP - BLK)
    subtract_trail()
    mine = pl.ds(pl.multiple_of(panel_index * BLK, BLK), BLK)
    factor_out[...] = front[:KSUP, mine]
    coupling_out[...] = front[KSUP:, mine]

    def pack(i, carry):
        second = i > panel_index
        top = pl.multiple_of(jnp.where(second, BLK, 0), BLK)
        start = pl.multiple_of(jnp.where(second, i - panel_index - 1, i) * BLK, BLK)
        blocks_out[pl.ds(pl.multiple_of(i * BLK, BLK), BLK), :] = trail[
            pl.ds(top, BLK), pl.ds(start, BLK)
        ]
        return carry

    lax.fori_loop(0, last + 2, pack, 0)


def separator_kernel(spot, blocks, shift, out, matrix, left, right, inverse_ref, factor_ref):
    size = SSEP // BLK
    share = 1.0 / 64
    row_ids = lax.broadcasted_iota(jnp.int32, (BLK, BLK), 0)
    col_ids = lax.broadcasted_iota(jnp.int32, (BLK, BLK), 1)
    for r in range(size):
        for c in range(size):
            span = (slice(r * BLK, (r + 1) * BLK), slice(c * BLK, (c + 1) * BLK))
            if c > r:
                matrix[span] = jnp.zeros((BLK, BLK), jnp.float32)
                continue
            p = min(r, size - 1 - r)
            i = c if r == p else p + 1 + c
            value = blocks[p, i * BLK : (i + 1) * BLK, :] * share
            if c == r:
                line = shift[r // 2, r % 2 : r % 2 + 1, :]
                value = value + jnp.where(row_ids == col_ids, line, 0.0)
            matrix[span] = value
    strips = [(t, t + 256, t + 256) for t in range(0, SSEP, 256)]
    factor_ref[...], inverse_ref[...] = factor_block(matrix[:BLK, :BLK])

    def step(j, carry):
        at = pl.multiple_of(j * BLK, BLK)
        inverse = inverse_ref[...]
        block = next_block(matrix, inverse, at)
        make_panel(matrix, inverse, factor_ref[...], left, right, at)
        subtract(matrix, left, right, strips)
        factor_ref[...], inverse_ref[...] = factor_block(block)
        return carry

    lax.fori_loop(0, size - 1, step, 0)
    matrix[: SSEP - BLK, SSEP - BLK :] = jnp.zeros((SSEP - BLK, BLK), jnp.float32)
    matrix[SSEP - BLK :, SSEP - BLK :] = factor_ref[...]
    top = pl.multiple_of(spot[0] * out.shape[0], out.shape[0])
    start = pl.multiple_of(spot[1] * out.shape[1], out.shape[1])
    out[...] = matrix[pl.ds(top, out.shape[0]), pl.ds(start, out.shape[1])]


def start_kernel(spot, subtree_of, design, cycle_index, outgoing, position, subtree_out):
    leaves, block_rows, _ = design.shape
    rows = leaves * block_rows
    subtree = subtree_of[spot[0]]
    subtree_out[0] = subtree
    index = cycle_index[pl.ds(pl.multiple_of(subtree * 8, 8), 8), :]
    position[...] = (index // rows) * block_rows + index % rows - subtree * block_rows

    def move(d, carry):
        outgoing[d] = design[subtree_of[d]]
        return carry

    lax.fori_loop(0, leaves, move, 0, unroll=8)


VM = pl.BlockSpec(memory_space=pltpu.VMEM)
SM = pl.BlockSpec(memory_space=pltpu.SMEM)
MESH = pl.DeviceIdType.MESH
Z, X, Y, LO = 8, 4, 4, 2


def place():
    leaf = lax.axis_index("leaf")
    panel = lax.axis_index("panel")
    z = leaf // (X * LO)
    x = leaf // LO % X
    y = panel // 2 * LO + leaf % LO
    return z, x, y, panel % 2


def device_at(z, x, y, core):
    return ((z * X + x) * LO + y % LO, y // LO * 2 + core)


def copy_to(source, target, sent, landed, device):
    return pltpu.make_async_remote_copy(
        src_ref=source, dst_ref=target, send_sem=sent, recv_sem=landed, device_id=device, device_id_type=MESH
    )


def greet(devices):
    barrier = pltpu.get_barrier_semaphore()
    for device in devices:
        pl.semaphore_signal(barrier, inc=1, device_id=device, device_id_type=MESH)
    pl.semaphore_wait(barrier, len(devices))


TILES = 18
STARTS = [15 * i // 7 for i in range(Z)]


def sum_kernel(
    blocks, shift, whole, shifts,
    landed_a, partial, landed_b, reduced, gathered,
    sent_a, got_a, sent_b, got_b, sent_c, got_c, local,
    sent_1, got_1, sent_2, got_2, sent_s, got_s, sent_h, got_h,
):
    z, x, y, core = place()
    lo, hi = y % LO, y // LO
    piece = TILES * 8
    half = piece // 2
    plane = [(dx, dy) for dx in range(X) for dy in range(LO) if dx or dy]

    def at_plane(dx, dy):
        return device_at(z, (x + dx) % X, hi * LO + (lo + dy) % LO, core)

    def at_z(d):
        return device_at((z + d) % Z, x, y, core)

    def at_y(d):
        return device_at(z, x, (y + d) % Y, core)

    def at_x(d):
        return device_at(z, (x + d) % X, y, core)

    sibling = device_at(z, x, y, 1 - core)
    greet(
        [at_plane(*d) for d in plane]
        + [at_z(d) for d in range(1, Z)]
        + [at_y(d) for d in range(1, Y)]
        + [sibling]
    )
    pending = []

    def go(copy):
        copy.start()
        pending.append(copy)
        return copy

    def rows_of(x_at, y_at):
        return pl.multiple_of((x_at * LO + y_at % LO) * piece, 8)

    def panel_of(y_at, core_at):
        return y_at // LO * 2 + core_at

    own_panel = panel_of(y, core)
    go(copy_to(shift, shifts.at[own_panel], sent_h.at[0], got_h.at[0], at_y(2)))
    go(copy_to(shift, shifts.at[own_panel], sent_h.at[1], got_h.at[1], sibling))
    keep = pltpu.make_async_copy(shift, shifts.at[own_panel], local.at[Z])
    keep.start()

    first = []
    for dx, dy in plane:
        i = dx * LO + dy
        at = rows_of((x + dx) % X, lo + dy)
        first.append(
            go(copy_to(blocks.at[pl.ds(at, piece), :], landed_a.at[i], sent_a.at[i], got_a.at[i], at_plane(dx, dy)))
        )
    total = blocks[pl.ds(rows_of(x, lo), piece), :]
    for (dx, dy), copy in zip(plane, first):
        copy.wait_recv()
        total = total + landed_a[dx * LO + dy]
    partial[...] = total

    def start_of(z_at):
        return pl.multiple_of(15 * z_at // 7 * 8, 8)

    second = []
    for d in range(1, Z):
        source = partial.at[pl.ds(start_of((z + d) % Z), 24), :]
        second.append(go(copy_to(source, landed_b.at[d], sent_b.at[d], got_b.at[d], at_z(d))))
    total = partial[pl.ds(start_of(z), 24), :]
    for d, copy in zip(range(1, Z), second):
        copy.wait_recv()
        total = total + landed_b[d]
    reduced[...] = total

    third = [
        go(copy_to(reduced, gathered.at[z], sent_c.at[d], got_c.at[d], at_z(d))) for d in range(1, Z)
    ]
    mine = pltpu.make_async_copy(reduced, gathered.at[z], local.at[0])
    mine.start()
    pending[0].wait_recv()
    go(copy_to(shifts.at[panel_of(y + 2 - y // 2 * 4, core)], shifts.at[panel_of(y + 2 - y // 2 * 4, core)],
               sent_h.at[2], got_h.at[2], sibling))
    mine.wait()
    for copy in third:
        copy.wait_recv()
    top = rows_of(x, y)
    own = whole.at[own_panel, pl.ds(top, piece), :]
    moves = []
    for i in range(Z):
        length = ((STARTS + [TILES])[i + 1] - STARTS[i]) * 8
        move = pltpu.make_async_copy(
            gathered.at[i, 0:length, :],
            whole.at[own_panel, pl.ds(pl.multiple_of(top + STARTS[i] * 8, 8), length), :],
            local.at[i],
        )
        move.start()
        moves.append(move)
    for move in moves:
        move.wait()

    def part(x_at, y_at, side, core_at=core):
        at = pl.multiple_of(rows_of(x_at, y_at) + side * half, 8)
        return whole.at[panel_of(y_at, core_at), pl.ds(at, half), :]

    def pass_on(ref, sems_sent, sems_got, index, device):
        return go(copy_to(ref, ref, sems_sent.at[index], sems_got.at[index], device))

    ring = [at_y, at_x]
    length = Y
    first_wave = {}
    for side in range(2):
        for d in range(1, length):
            first_wave[side, d] = pass_on(part(x, y, side), sent_1, got_1, side * 4 + d, ring[side](d))
    second_wave = []

    def spread(side, d):
        where = part(x, (y - d) % Y, 0) if side == 0 else part((x - d) % X, y, 1)
        for e in range(1, length):
            second_wave.append(
                (side, d, e, pass_on(where, sent_2, got_2, (side * 4 + d) * 4 + e, ring[1 - side](e)))
            )
        pass_on(where, sent_s, got_s, (side * 4 + d) * 4, sibling)

    for side in range(2):
        spread(side, 0)
    for d in range(1, length):
        for side in range(2):
            first_wave[side, d].wait_recv()
            spread(side, d)
    for side, d, e, copy in second_wave:
        copy.wait_recv()
        if side == 0:
            where = part((x - e) % X, (y - d) % Y, 0)
        else:
            where = part((x - d) % X, (y - e) % Y, 1)
        pass_on(where, sent_s, got_s, (side * 4 + d) * 4 + e, sibling)
    for copy in pending:
        copy.wait_send()
    for side in range(2):
        for d in range(length):
            for e in range(length):
                if side == 0:
                    where = part((x - e) % X, (y - d) % Y, 0, 1 - core)
                else:
                    where = part((x - d) % X, (y - e) % Y, 1, 1 - core)
                index = (side * 4 + d) * 4 + e
                copy_to(where, where, sent_s.at[index], got_s.at[index], sibling).wait_recv()
    keep.wait()
    for i, panel in ((1, panel_of(y, 1 - core)), (2, panel_of(y + 2 - y // 2 * 4, 1 - core))):
        copy_to(shift, shifts.at[panel], sent_h.at[i], got_h.at[i], sibling).wait_recv()


def sum_blocks(blocks, shift):
    rows = blocks.shape[0]
    dma = pltpu.SemaphoreType.DMA
    f32 = jnp.float32
    return pl.pallas_call(
        sum_kernel,
        out_shape=(
            jax.ShapeDtypeStruct((4, rows, BLK), f32),
            jax.ShapeDtypeStruct((4, 2, BLK), f32),
        ),
        in_specs=[VM, VM],
        out_specs=(VM, VM),
        scratch_shapes=[
            pltpu.VMEM((8, TILES * 8, BLK), f32),
            pltpu.VMEM((TILES * 8, BLK), f32),
            pltpu.VMEM((Z, 24, BLK), f32),
            pltpu.VMEM((24, BLK), f32),
            pltpu.VMEM((Z, 24, BLK), f32),
            dma((8,)), dma((8,)), dma((8,)), dma((8,)), dma((8,)), dma((8,)), dma((Z + 1,)),
            dma((8,)), dma((8,)), dma((32,)), dma((32,)), dma((32,)), dma((32,)), dma((3,)), dma((3,)),
        ],
        compiler_params=pltpu.CompilerParams(collective_id=1, has_side_effects=True, vmem_limit_bytes=40 << 20),
        name="separator_sum",
    )(blocks, shift)


ORDER = (0, 1, 7, 2, 6, 3, 5, 4)


def relay(along, dz, slab, go, sent_s, got_s, sibling):
    for d in (1, 3, 2):
        along[dz, d].wait_recv()
        i = dz * Y + d
        go(copy_to(slab(dz, d), slab(dz, d), sent_s.at[i], got_s.at[i], sibling))


def row_pattern(subtree, position, fill):
    count, lanes = position.shape
    rows = count * lanes
    here = lax.broadcasted_iota(jnp.int32, (rows, lanes), 0)
    chosen = jnp.concatenate(
        [jnp.where(here == position[b : b + 1, :], 1.0, 0.0) for b in range(count)], 1
    ).astype(jnp.bfloat16)
    blocks = fill.shape[1]
    source = lax.broadcasted_iota(jnp.int32, (blocks, rows), 0)
    wanted = subtree * count + lax.broadcasted_iota(jnp.int32, (blocks, rows), 1) // lanes
    pick = jnp.where(source == wanted, 1.0, 0.0).astype(jnp.bfloat16)
    lines = jnp.dot(fill[...].astype(jnp.bfloat16), pick, preferred_element_type=jnp.float32)
    return dot_nt(chosen, lines.astype(jnp.bfloat16), None)


def exchange_kernel(
    outgoing, position, subtree, fill, design, touch,
    middle, local, sent_a, got_a, sent_y, got_y, sent_s, got_s,
):
    z, x, y, core = place()
    own_panel = y // LO * 2 + core
    sibling = device_at(z, x, y, 1 - core)
    near = [(dz, dx) for dz in ORDER for dx in range(X) if dz or dx]

    def at(dz, dx):
        return device_at((z + dz) % Z, (x + dx) % X, y, core)

    def at_y(d):
        return device_at(z, x, (y + d) % Y, core)

    greet([at(*d) for d in near] + [at_y(d) for d in range(1, Y)] + [sibling])
    pending = []

    def go(copy):
        copy.start()
        pending.append(copy)
        return copy

    arrive = {}
    keep = pltpu.make_async_copy(outgoing.at[z, x], middle.at[z, x], local.at[Z])
    keep.start()
    for dz, dx in near:
        i = dz * X + dx
        arrive[dz, dx] = go(
            copy_to(
                outgoing.at[(z + dz) % Z, (x + dx) % X], middle.at[z, x], sent_a.at[i], got_a.at[i], at(dz, dx)
            )
        )
    touch[...] = row_pattern(subtree[0], position[...], fill)
    along = {}
    moves = []

    def slab(dz, d):
        y_from = (y - d) % Y
        return design.at[y_from // LO * 2 + core, (z - dz) % Z, :, y_from % LO]

    for n, dz in enumerate(ORDER):
        for dx in range(X):
            if dz or dx:
                arrive[dz, dx].wait_recv()
        if dz == 0:
            keep.wait()
        z_from = (z - dz) % Z
        target = design.at[own_panel, z_from, :, y % LO]
        other = middle.at[z_from, :, 1 - y % LO]
        same = middle.at[z_from, :, y % LO]
        for d in (2, 1, 3):
            source = same if d == 2 else other
            i = dz * Y + d
            along[dz, d] = go(copy_to(source, target, sent_y.at[i], got_y.at[i], at_y(d)))
        go(copy_to(same, target, sent_s.at[dz * Y], got_s.at[dz * Y], sibling))
        move = pltpu.make_async_copy(same, target, local.at[dz])
        move.start()
        moves.append(move)
        if n:
            relay(along, ORDER[n - 1], slab, go, sent_s, got_s, sibling)
    relay(along, ORDER[-1], slab, go, sent_s, got_s, sibling)
    for copy in pending:
        copy.wait_send()
    for move in moves:
        move.wait()
    for dz in ORDER:
        for d in range(Y):
            i = dz * Y + d
            copy_to(slab(dz, d), slab(dz, d), sent_s.at[i], got_s.at[i], sibling).wait_recv()


def exchange(outgoing, position, subtree, fill):
    dma = pltpu.SemaphoreType.DMA
    rows, piece = outgoing.shape[-2:]
    return pl.pallas_call(
        exchange_kernel,
        out_shape=(
            jax.ShapeDtypeStruct((4,) + outgoing.shape, outgoing.dtype),
            jax.ShapeDtypeStruct((position.size, fill.shape[0]), jnp.float32),
        ),
        in_specs=[VM, VM, SM, VM],
        out_specs=(VM, VM),
        scratch_shapes=[pltpu.VMEM(outgoing.shape, outgoing.dtype), dma((Z + 1,))]
        + [dma((Z * X,)) for _ in range(6)],
        compiler_params=pltpu.CompilerParams(collective_id=2, has_side_effects=True, vmem_limit_bytes=40 << 20),
        name="design_exchange",
    )(outgoing, position, subtree, fill)


def per_device(
    pix_cycle, cycle_to_dissection, subtree_of, fill_blocks, leaf_shift, separator_shift
):
    leaves = lax.axis_size("leaf")
    panels = lax.axis_size("panel")
    rows, piece = pix_cycle.shape
    block_rows = rows // leaves
    leaf_index = lax.axis_index("leaf")
    panel_index = lax.axis_index("panel")
    outgoing, position, subtree = pl.pallas_call(
        start_kernel,
        out_shape=(
            jax.ShapeDtypeStruct((leaves, block_rows, piece), pix_cycle.dtype),
            jax.ShapeDtypeStruct((8, BLK), jnp.int32),
            jax.ShapeDtypeStruct((1,), jnp.int32),
        ),
        in_specs=[SM, SM, VM, VM],
        out_specs=(VM, VM, SM),
        compiler_params=pltpu.CompilerParams(vmem_limit_bytes=VMEM_LIMIT),
        name="start_rows",
    )(
        leaf_index[None],
        subtree_of,
        pix_cycle.reshape(leaves, block_rows, piece),
        cycle_to_dissection.reshape(-1, BLK),
    )
    received, touch = exchange(
        outgoing.reshape(Z, X, LO, block_rows, piece), position, subtree, fill_blocks.T
    )
    design = received.reshape(panels, rows, piece)
    count = SSEP // BLK + 1
    factor_cols, coupling_cols, blocks = pl.pallas_call(
        leaf_kernel,
        out_shape=(
            jax.ShapeDtypeStruct((KSUP, KSUP // panels), jnp.float32),
            jax.ShapeDtypeStruct((SSEP, KSUP // panels), jnp.float32),
            jax.ShapeDtypeStruct((count * BLK, BLK), jnp.float32),
        ),
        in_specs=[SM, VM, VM, VM],
        out_specs=(VM, VM, VM),
        scratch_shapes=[
            pltpu.VMEM((rows, FRONT), jnp.bfloat16),
            pltpu.VMEM((FRONT, KSUP), jnp.float32),
            pltpu.VMEM((FRONT, 6 * BLK), jnp.bfloat16),
            pltpu.VMEM((FRONT, 6 * BLK), jnp.bfloat16),
            pltpu.VMEM((2 * BLK, SSEP), jnp.float32),
            pltpu.VMEM((BLK, BLK), jnp.float32),
            pltpu.VMEM((BLK, BLK), jnp.float32),
            pltpu.VMEM((1, FRONT), jnp.float32),
        ],
        compiler_params=pltpu.CompilerParams(vmem_limit_bytes=VMEM_LIMIT),
        name="leaf_front",
    )(jnp.stack([panel_index, subtree[0]]), design, touch, leaf_shift)
    whole, shifts = sum_blocks(blocks, separator_shift.reshape(2, BLK))
    result_rows = pl.pallas_call(
        separator_kernel,
        out_shape=jax.ShapeDtypeStruct((SSEP // leaves, SSEP // panels), jnp.float32),
        in_specs=[SM, VM, VM],
        out_specs=VM,
        scratch_shapes=[
            pltpu.VMEM((SSEP, SSEP), jnp.float32),
            pltpu.VMEM((SSEP, 6 * BLK), jnp.bfloat16),
            pltpu.VMEM((SSEP, 6 * BLK), jnp.bfloat16),
            pltpu.VMEM((BLK, BLK), jnp.float32),
            pltpu.VMEM((BLK, BLK), jnp.float32),
        ],
        compiler_params=pltpu.CompilerParams(vmem_limit_bytes=VMEM_LIMIT),
        name="separator_front",
    )(jnp.stack([leaf_index, panel_index]), whole, shifts)
    return (factor_cols, coupling_cols, result_rows)


def solution(mesh):
    placed = (P("leaf", "panel"), P(), P(), P(), P(), P("panel"))
    return jax.shard_map(
        per_device,
        mesh=mesh,
        in_specs=placed,
        out_specs=(P("leaf", "panel"), P("leaf", "panel"), P("leaf", "panel")),
        check_vma=False,
    )
```

```python
import jax
import jax.numpy as jnp
from jax import lax
from jax.experimental import pallas as pl
from jax.experimental.pallas import tpu as pltpu
from jax.sharding import PartitionSpec as P

KSUP = 512
SSEP = 1024
FRONT = KSUP + SSEP
BLK = 128
SLAB = 16
HIGHEST = lax.Precision.HIGHEST
VMEM_LIMIT = 26 << 20


def row_of(values, index):
    return jnp.broadcast_to(values[index : index + 1, :], (8, BLK))


def twice(values):
    return jnp.concatenate([values, values], 0)


def factor_block(block):
    lanes8 = lax.broadcasted_iota(jnp.int32, (8, BLK), 1)
    lanes = lax.broadcasted_iota(jnp.int32, (SLAB, BLK), 1)
    subs = lax.broadcasted_iota(jnp.int32, (SLAB, BLK), 0)
    count = BLK // SLAB
    work = [block[SLAB * s : SLAB * (s + 1), :] for s in range(count)]
    scaled = [None] * count
    corner = [None] * count
    for s in range(count):
        base = SLAB * s
        own = work[s]
        inside = (lanes >= base) & (lanes < base + SLAB)
        cols = []
        for j in range(SLAB):
            first = 8 if j >= 8 else 0
            cols.append(jnp.broadcast_to(own[first:, base + j : base + j + 1], (SLAB - first, BLK)))
        below = {
            b: [
                jnp.broadcast_to(work[b][:, base + j : base + j + 1], (SLAB, BLK))
                for j in range(SLAB)
            ]
            for b in range(s + 1, count)
        }
        start = jnp.where(inside, jnp.where(lanes - base == subs, 1.0, 0.0), own)
        rows = [row_of(start, j) for j in range(SLAB)]
        inv_pivot, scale, mult = [], [], {}
        for k in range(SLAB):
            off = 8 if k >= 8 else 0
            pivot = row_of(cols[k], k - off)
            inverse = 1.0 / pivot
            inv_pivot.append(inverse)
            scale.append(lax.rsqrt(pivot))
            for j in range(k + 1, SLAB):
                mult[k, j] = row_of(cols[k], j - off) * inverse
            for j in range(k + 1, SLAB):
                if j >= 8:
                    source = cols[k] if k >= 8 else cols[k][8:, :]
                    cols[j] = cols[j] - source * mult[k, j]
                else:
                    cols[j] = cols[j] - cols[k] * twice(mult[k, j])
                rows[j] = rows[j] - mult[k, j] * rows[k]
        solved = [rows[k] * inv_pivot[k] for k in range(SLAB)]
        for i in reversed(range(SLAB)):
            for k in range(i):
                solved[k] = solved[k] - mult[k, i] * solved[i]
        for b in range(s + 1, count):
            rest = jnp.where(inside, 0.0, work[b])
            for k in reversed(range(SLAB)):
                rest = rest - below[b][k] * twice(solved[k])
            work[b] = rest
        out = jnp.zeros((SLAB, BLK), jnp.float32)
        low = jnp.zeros((SLAB, BLK), jnp.float32)
        for k in range(SLAB):
            out = jnp.where(subs == k, twice(rows[k] * scale[k]), out)
            if k >= 8:
                column = jnp.concatenate(
                    [jnp.zeros((8, BLK), jnp.float32), cols[k] * scale[k]], 0
                )
            else:
                column = cols[k] * twice(scale[k])
            low = jnp.where((lanes == base + k) & (subs >= k), column, low)
        scaled[s] = out
        corner[s] = low
    full = jnp.concatenate(scaled, 0)
    corners = jnp.concatenate(corner, 0)
    row_ids = lax.broadcasted_iota(jnp.int32, (BLK, BLK), 0)
    col_ids = lax.broadcasted_iota(jnp.int32, (BLK, BLK), 1)
    factor = jnp.where(row_ids // SLAB > col_ids // SLAB, full.T, corners)
    inverse = jnp.where(row_ids >= col_ids, full, 0.0)
    return factor, inverse


def dot_nt(a, b, precision=HIGHEST):
    return lax.dot_general(
        a, b, (((1,), (1,)), ((), ())), precision=precision, preferred_element_type=jnp.float32
    )


def dot_tn(a, b):
    return lax.dot_general(a, b, (((0,), (0,)), ((), ())), preferred_element_type=jnp.float32)


def split_parts(values):
    high = values.astype(jnp.bfloat16)
    rest = values - high.astype(jnp.float32)
    middle = rest.astype(jnp.bfloat16)
    low = (rest - middle.astype(jnp.float32)).astype(jnp.bfloat16)
    left = jnp.concatenate([high, middle, high, middle, high, low], 1)
    right = jnp.concatenate([high, high, middle, middle, low, high], 1)
    return left, right


def make_panel(matrix, inverse, factor, left, right, at):
    rows = matrix.shape[0]
    panel = dot_nt(matrix[:, pl.ds(at, BLK)], inverse)
    row_ids = lax.broadcasted_iota(jnp.int32, (rows, BLK), 0)
    panel = jnp.where(row_ids >= at + BLK, panel, 0.0)
    left[...], right[...] = split_parts(panel)
    matrix[:, pl.ds(at, BLK)] = panel
    matrix[pl.ds(at, BLK), pl.ds(at, BLK)] = factor


def next_block(matrix, inverse, at):
    after = pl.multiple_of(at + BLK, BLK)
    head = dot_nt(matrix[pl.ds(after, BLK), pl.ds(at, BLK)], inverse)
    return matrix[pl.ds(after, BLK), pl.ds(after, BLK)] - dot_nt(head, head)


def subtract(matrix, left, right, strips):
    for top, bottom, width in strips:
        matrix[top:bottom, :width] = matrix[top:bottom, :width] - dot_nt(
            left[top:bottom, :], right[:width, :], None
        )


def leaf_kernel(
    subtree_of, design, touch, shift_rows, factor_out, coupling_out, blocks_out,
    masked, front, left, right, trail, inverse_ref, factor_ref, shift,
):
    panel_index = lax.axis_index("panel")
    subtree = subtree_of[lax.axis_index("leaf")]
    rows = design.shape[1]
    piece = design.shape[2]
    shift[...] = shift_rows[pl.ds(subtree, 1), :]
    for c in range(FRONT // BLK):
        p, at = c * BLK // piece, c * BLK % piece
        keep = jnp.broadcast_to(touch[:, c : c + 1], (rows, BLK)).astype(jnp.bfloat16)
        masked[:, c * BLK : (c + 1) * BLK] = design[p, :, at : at + BLK] * keep
    scale = 1.0 / rows
    for top in range(0, FRONT, 512):
        front[top : top + 512, :] = dot_tn(masked[:, top : top + 512], masked[:, :KSUP]) * scale
    row_ids = lax.broadcasted_iota(jnp.int32, (BLK, BLK), 0)
    col_ids = lax.broadcasted_iota(jnp.int32, (BLK, BLK), 1)
    same = row_ids == col_ids
    for b in range(KSUP // BLK):
        span = slice(b * BLK, (b + 1) * BLK)
        front[span, span] = front[span, span] + jnp.where(same, shift[:, span], 0.0)
    last = SSEP // BLK - 1
    halves = (panel_index, last - panel_index)
    for h, block_row in enumerate(halves):
        at = pl.multiple_of(KSUP + block_row * BLK, BLK)
        trail[h * BLK : (h + 1) * BLK, :] = (
            dot_tn(masked[:, pl.ds(at, BLK)], masked[:, KSUP:]) * scale
        )
        corner = pl.ds(pl.multiple_of(block_row * BLK, BLK), BLK)
        span = slice(h * BLK, (h + 1) * BLK)
        line = shift[:, pl.ds(at, BLK)]
        trail[span, corner] = trail[span, corner] + jnp.where(same, line, 0.0)

    def subtract_trail():
        for h, block_row in enumerate(halves):
            at = pl.multiple_of(KSUP + block_row * BLK, BLK)
            span = slice(h * BLK, (h + 1) * BLK)
            trail[span, :] = trail[span, :] - dot_nt(left[pl.ds(at, BLK), :], right[KSUP:, :], None)

    factor_ref[...], inverse_ref[...] = factor_block(front[:BLK, :BLK])

    def step(j, carry):
        at = pl.multiple_of(j * BLK, BLK)
        inverse = inverse_ref[...]
        block = next_block(front, inverse, at)
        make_panel(front, inverse, factor_ref[...], left, right, at)
        subtract(front, left, right, [(BLK, 256, 256), (256, FRONT, KSUP)])
        subtract_trail()
        factor_ref[...], inverse_ref[...] = factor_block(block)
        return carry

    lax.fori_loop(0, KSUP // BLK - 1, step, 0)
    make_panel(front, inverse_ref[...], factor_ref[...], left, right, KSUP - BLK)
    subtract_trail()
    mine = pl.ds(pl.multiple_of(panel_index * BLK, BLK), BLK)
    factor_out[...] = front[:KSUP, mine]
    coupling_out[...] = front[KSUP:, mine]

    def pack(i, carry):
        second = i > panel_index
        top = pl.multiple_of(jnp.where(second, BLK, 0), BLK)
        start = pl.multiple_of(jnp.where(second, i - panel_index - 1, i) * BLK, BLK)
        blocks_out[pl.ds(pl.multiple_of(i * BLK, BLK), BLK), :] = trail[
            pl.ds(top, BLK), pl.ds(start, BLK)
        ]
        return carry

    lax.fori_loop(0, last + 2, pack, 0)


def separator_kernel(blocks, shift, out, matrix, left, right, inverse_ref, factor_ref):
    size = SSEP // BLK
    share = 1.0 / 64
    row_ids = lax.broadcasted_iota(jnp.int32, (BLK, BLK), 0)
    col_ids = lax.broadcasted_iota(jnp.int32, (BLK, BLK), 1)
    for r in range(size):
        for c in range(size):
            span = (slice(r * BLK, (r + 1) * BLK), slice(c * BLK, (c + 1) * BLK))
            if c > r:
                matrix[span] = jnp.zeros((BLK, BLK), jnp.float32)
                continue
            p = min(r, size - 1 - r)
            i = c if r == p else p + 1 + c
            value = blocks[p, i * BLK : (i + 1) * BLK, :] * share
            if c == r:
                line = shift[r // 2, r % 2 : r % 2 + 1, :]
                value = value + jnp.where(row_ids == col_ids, line, 0.0)
            matrix[span] = value
    strips = [(t, t + 256, t + 256) for t in range(0, SSEP, 256)]
    factor_ref[...], inverse_ref[...] = factor_block(matrix[:BLK, :BLK])

    def step(j, carry):
        at = pl.multiple_of(j * BLK, BLK)
        inverse = inverse_ref[...]
        block = next_block(matrix, inverse, at)
        make_panel(matrix, inverse, factor_ref[...], left, right, at)
        subtract(matrix, left, right, strips)
        factor_ref[...], inverse_ref[...] = factor_block(block)
        return carry

    lax.fori_loop(0, size - 1, step, 0)
    matrix[: SSEP - BLK, SSEP - BLK :] = jnp.zeros((SSEP - BLK, BLK), jnp.float32)
    matrix[SSEP - BLK :, SSEP - BLK :] = factor_ref[...]
    top = pl.multiple_of(lax.axis_index("leaf") * out.shape[0], out.shape[0])
    start = pl.multiple_of(lax.axis_index("panel") * out.shape[1], out.shape[1])
    out[...] = matrix[pl.ds(top, out.shape[0]), pl.ds(start, out.shape[1])]


VM = pl.BlockSpec(memory_space=pltpu.VMEM)
SM = pl.BlockSpec(memory_space=pltpu.SMEM)
MESH = pl.DeviceIdType.MESH
Z, X, Y, LO = 8, 4, 4, 2


def place():
    leaf = lax.axis_index("leaf")
    panel = lax.axis_index("panel")
    z = leaf // (X * LO)
    x = leaf // LO % X
    y = panel // 2 * LO + leaf % LO
    return z, x, y, panel % 2


def device_at(z, x, y, core):
    return ((z * X + x) * LO + y % LO, y // LO * 2 + core)


def copy_to(source, target, sent, landed, device):
    return pltpu.make_async_remote_copy(
        src_ref=source, dst_ref=target, send_sem=sent, recv_sem=landed, device_id=device, device_id_type=MESH
    )


def greet(devices, meanwhile=None):
    barrier = pltpu.get_barrier_semaphore()
    for device in devices:
        pl.semaphore_signal(barrier, inc=1, device_id=device, device_id_type=MESH)
    if meanwhile is not None:
        meanwhile()
    pl.semaphore_wait(barrier, len(devices))


TILES = 9
CHUNK = 16


def sum_kernel(
    blocks, shift, whole, shifts,
    landed_a, partial, landed_b, reduced, gathered,
    sent_a, got_a, sent_b, got_b, sent_c, got_c, local,
    sent_1, got_1, sent_2, got_2, sent_s, got_s, sent_h, got_h,
):
    z, x, y, core = place()
    lo, hi = y % LO, y // LO
    half = TILES * 8
    piece = 2 * half
    plane = [(dx, dy) for dx in range(X) for dy in range(LO) if dx or dy]

    def at_plane(dx, dy):
        return device_at(z, (x + dx) % X, hi * LO + (lo + dy) % LO, core)

    def at_z(d):
        return device_at((z + d) % Z, x, y, core)

    def at_y(d):
        return device_at(z, x, (y + d) % Y, core)

    def at_x(d):
        return device_at(z, (x + d) % X, y, core)

    sibling = device_at(z, x, y, 1 - core)
    greet(
        [at_plane(*d) for d in plane]
        + [at_z(d) for d in range(1, Z)]
        + [at_y(d) for d in range(1, Y)]
        + [sibling]
    )
    pending = []

    def go(copy):
        copy.start()
        pending.append(copy)
        return copy

    def rows_of(x_at, y_at, side=0):
        return pl.multiple_of((x_at * LO + y_at % LO) * piece + side * half, 8)

    def panel_of(y_at, core_at):
        return y_at // LO * 2 + core_at

    first = {}
    for side in range(2):
        for dx, dy in plane:
            i = side * 8 + dx * LO + dy
            at = rows_of((x + dx) % X, lo + dy, side)
            first[side, dx, dy] = go(
                copy_to(
                    blocks.at[pl.ds(at, half), :], landed_a.at[i], sent_a.at[i], got_a.at[i], at_plane(dx, dy)
                )
            )

    own_panel = panel_of(y, core)
    over = go(copy_to(shift, shifts.at[own_panel], sent_h.at[0], got_h.at[0], at_y(2)))
    go(copy_to(shift, shifts.at[own_panel], sent_h.at[1], got_h.at[1], sibling))
    keep = pltpu.make_async_copy(shift, shifts.at[own_panel], local.at[2 * Z])
    keep.start()

    def start_of(z_at):
        return pl.multiple_of(z_at % Z * 8, 8)

    second = {}
    for side in range(2):
        total = blocks[pl.ds(rows_of(x, lo, side), half), :]
        for dx, dy in plane:
            first[side, dx, dy].wait_recv()
            total = total + landed_a[side * 8 + dx * LO + dy]
        partial[side] = total
        for d in range(1, Z):
            i = side * Z + d
            source = partial.at[side, pl.ds(start_of(z + d), CHUNK), :]
            second[side, d] = go(copy_to(source, landed_b.at[i], sent_b.at[i], got_b.at[i], at_z(d)))

    third, mine = {}, []
    for side in range(2):
        total = partial[side, pl.ds(start_of(z), CHUNK), :]
        for d in range(1, Z):
            second[side, d].wait_recv()
            total = total + landed_b[side * Z + d]
        reduced[side] = total
        for d in range(1, Z):
            i = side * Z + d
            third[side, d] = go(
                copy_to(reduced.at[side], gathered.at[side, z], sent_c.at[i], got_c.at[i], at_z(d))
            )
        move = pltpu.make_async_copy(reduced.at[side], gathered.at[side, z], local.at[side * Z])
        move.start()
        mine.append(move)
    over.wait_recv()
    far = shifts.at[panel_of(y + 2 - y // 2 * 4, core)]
    go(copy_to(far, far, sent_h.at[2], got_h.at[2], sibling))

    def assemble(side):
        mine[side].wait()
        for d in range(1, Z):
            third[side, d].wait_recv()
        top = rows_of(x, y, side)
        moves = []
        for i in range(Z):
            length = CHUNK if i == Z - 1 else 8
            moves.append(
                pltpu.make_async_copy(
                    gathered.at[side, i, 0:length, :],
                    whole.at[own_panel, pl.ds(pl.multiple_of(top + i * 8, 8), length), :],
                    local.at[side * Z + i],
                )
            )
            moves[-1].start()
        for move in moves:
            move.wait()

    def part(x_at, y_at, side, core_at=core):
        at = pl.multiple_of(rows_of(x_at, y_at) + side * half, 8)
        return whole.at[panel_of(y_at, core_at), pl.ds(at, half), :]

    def pass_on(ref, sems_sent, sems_got, index, device):
        return go(copy_to(ref, ref, sems_sent.at[index], sems_got.at[index], device))

    ring = [at_y, at_x]
    length = Y
    first_wave = {}
    second_wave = []

    def spread(side, d):
        where = part(x, (y - d) % Y, 0) if side == 0 else part((x - d) % X, y, 1)
        for e in range(1, length):
            second_wave.append(
                (side, d, e, pass_on(where, sent_2, got_2, (side * 4 + d) * 4 + e, ring[1 - side](e)))
            )
        pass_on(where, sent_s, got_s, (side * 4 + d) * 4, sibling)

    for side in range(2):
        assemble(side)
        for d in range(1, length):
            first_wave[side, d] = pass_on(part(x, y, side), sent_1, got_1, side * 4 + d, ring[side](d))
        spread(side, 0)
    for d in range(1, length):
        for side in range(2):
            first_wave[side, d].wait_recv()
            spread(side, d)
    for side, d, e, copy in second_wave:
        copy.wait_recv()
        if side == 0:
            where = part((x - e) % X, (y - d) % Y, 0)
        else:
            where = part((x - d) % X, (y - e) % Y, 1)
        pass_on(where, sent_s, got_s, (side * 4 + d) * 4 + e, sibling)
    for copy in pending:
        copy.wait_send()
    for side in range(2):
        for d in range(length):
            for e in range(length):
                if side == 0:
                    where = part((x - e) % X, (y - d) % Y, 0, 1 - core)
                else:
                    where = part((x - d) % X, (y - e) % Y, 1, 1 - core)
                index = (side * 4 + d) * 4 + e
                copy_to(where, where, sent_s.at[index], got_s.at[index], sibling).wait_recv()
    keep.wait()
    for i, panel in ((1, panel_of(y, 1 - core)), (2, panel_of(y + 2 - y // 2 * 4, 1 - core))):
        copy_to(shift, shifts.at[panel], sent_h.at[i], got_h.at[i], sibling).wait_recv()


def sum_blocks(blocks, shift):
    rows = blocks.shape[0]
    dma = pltpu.SemaphoreType.DMA
    f32 = jnp.float32
    return pl.pallas_call(
        sum_kernel,
        out_shape=(
            jax.ShapeDtypeStruct((4, rows, BLK), f32),
            jax.ShapeDtypeStruct((4, 2, BLK), f32),
        ),
        in_specs=[VM, VM],
        out_specs=(VM, VM),
        scratch_shapes=[
            pltpu.VMEM((16, TILES * 8, BLK), f32),
            pltpu.VMEM((2, TILES * 8, BLK), f32),
            pltpu.VMEM((2 * Z, CHUNK, BLK), f32),
            pltpu.VMEM((2, CHUNK, BLK), f32),
            pltpu.VMEM((2, Z, CHUNK, BLK), f32),
            dma((16,)), dma((16,)), dma((16,)), dma((16,)), dma((16,)), dma((16,)), dma((2 * Z + 1,)),
            dma((8,)), dma((8,)), dma((32,)), dma((32,)), dma((32,)), dma((32,)), dma((3,)), dma((3,)),
        ],
        compiler_params=pltpu.CompilerParams(collective_id=1, has_side_effects=True, vmem_limit_bytes=16 << 20),
        name="separator_sum",
    )(blocks, shift)


ORDER = (0, 1, 7, 2, 6, 3, 5, 4)


def relay(along, dz, slab, go, sent_s, got_s, sibling):
    for d in (1, 3, 2):
        along[dz, d].wait_recv()
        i = dz * Y + d
        go(copy_to(slab(dz, d), slab(dz, d), sent_s.at[i], got_s.at[i], sibling))


def row_pattern(subtree, position, fill):
    count, lanes = position.shape
    rows = count * lanes
    here = lax.broadcasted_iota(jnp.int32, (rows, lanes), 0)
    chosen = jnp.concatenate(
        [jnp.where(here == position[b : b + 1, :], 1.0, 0.0) for b in range(count)], 1
    ).astype(jnp.bfloat16)
    blocks = fill.shape[1]
    source = lax.broadcasted_iota(jnp.int32, (blocks, rows), 0)
    wanted = subtree * count + lax.broadcasted_iota(jnp.int32, (blocks, rows), 1) // lanes
    pick = jnp.where(source == wanted, 1.0, 0.0).astype(jnp.bfloat16)
    lines = jnp.dot(fill[...].astype(jnp.bfloat16), pick, preferred_element_type=jnp.float32)
    return dot_nt(chosen, lines.astype(jnp.bfloat16), None)


def exchange_kernel(
    subtree_of, start, cycle_index, fill, design, touch,
    outgoing, middle, local, sent_a, got_a, sent_y, got_y, sent_s, got_s,
):
    z, x, y, core = place()
    own_panel = y // LO * 2 + core
    sibling = device_at(z, x, y, 1 - core)
    near = [(dz, dx) for dz in ORDER for dx in range(X) if dz or dx]

    def at(dz, dx):
        return device_at((z + dz) % Z, (x + dx) % X, y, core)

    def at_y(d):
        return device_at(z, x, (y + d) % Y, core)

    def order_blocks():
        for d in range(Z * X * LO):
            outgoing[d // (X * LO), d // LO % X, d % LO] = start[subtree_of[d]]

    greet([at(*d) for d in near] + [at_y(d) for d in range(1, Y)] + [sibling], order_blocks)
    pending = []

    def go(copy):
        copy.start()
        pending.append(copy)
        return copy

    arrive = {}
    keep = pltpu.make_async_copy(outgoing.at[z, x], middle.at[z, x], local.at[Z])
    keep.start()
    for dz, dx in near:
        i = dz * X + dx
        arrive[dz, dx] = go(
            copy_to(
                outgoing.at[(z + dz) % Z, (x + dx) % X], middle.at[z, x], sent_a.at[i], got_a.at[i], at(dz, dx)
            )
        )
    block_rows = start.shape[1]
    rows = start.shape[0] * block_rows
    subtree = subtree_of[lax.axis_index("leaf")]
    index = cycle_index[subtree]
    position = (index // rows) * block_rows + index % rows - subtree * block_rows
    touch[...] = row_pattern(subtree, position, fill)
    along = {}
    moves = []

    def slab(dz, d):
        y_from = (y - d) % Y
        return design.at[y_from // LO * 2 + core, (z - dz) % Z, :, y_from % LO]

    for n, dz in enumerate(ORDER):
        for dx in range(X):
            if dz or dx:
                arrive[dz, dx].wait_recv()
        if dz == 0:
            keep.wait()
        z_from = (z - dz) % Z
        target = design.at[own_panel, z_from, :, y % LO]
        other = middle.at[z_from, :, 1 - y % LO]
        same = middle.at[z_from, :, y % LO]
        for d in (2, 1, 3):
            source = same if d == 2 else other
            i = dz * Y + d
            along[dz, d] = go(copy_to(source, target, sent_y.at[i], got_y.at[i], at_y(d)))
        go(copy_to(same, target, sent_s.at[dz * Y], got_s.at[dz * Y], sibling))
        move = pltpu.make_async_copy(same, target, local.at[dz])
        move.start()
        moves.append(move)
        if n:
            relay(along, ORDER[n - 1], slab, go, sent_s, got_s, sibling)
    relay(along, ORDER[-1], slab, go, sent_s, got_s, sibling)
    for copy in pending:
        copy.wait_send()
    for move in moves:
        move.wait()
    for dz in ORDER:
        for d in range(Y):
            i = dz * Y + d
            copy_to(slab(dz, d), slab(dz, d), sent_s.at[i], got_s.at[i], sibling).wait_recv()


def exchange(subtree_of, start, cycle_index, fill):
    dma = pltpu.SemaphoreType.DMA
    shape = (Z, X, LO) + start.shape[1:]
    return pl.pallas_call(
        exchange_kernel,
        out_shape=(
            jax.ShapeDtypeStruct((4,) + shape, start.dtype),
            jax.ShapeDtypeStruct((cycle_index.size // start.shape[0], fill.shape[0]), jnp.float32),
        ),
        in_specs=[SM, VM, VM, VM],
        out_specs=(VM, VM),
        scratch_shapes=[
            pltpu.VMEM(shape, start.dtype),
            pltpu.VMEM(shape, start.dtype),
            dma((Z + 1,)),
        ]
        + [dma((Z * X,)) for _ in range(6)],
        compiler_params=pltpu.CompilerParams(
            collective_id=2, has_side_effects=True, vmem_limit_bytes=20 << 20
        ),
        name="design_exchange",
    )(subtree_of, start, cycle_index, fill)


def per_device(
    pix_cycle, cycle_to_dissection, subtree_of, fill_blocks, leaf_shift, separator_shift
):
    leaves = lax.axis_size("leaf")
    panels = lax.axis_size("panel")
    rows, piece = pix_cycle.shape
    block_rows = rows // leaves
    received, touch = exchange(
        subtree_of,
        pix_cycle.reshape(leaves, block_rows, piece),
        cycle_to_dissection.reshape(leaves, rows // BLK, BLK),
        fill_blocks.T,
    )
    design = received.reshape(panels, rows, piece)
    count = SSEP // BLK + 1
    factor_cols, coupling_cols, blocks = pl.pallas_call(
        leaf_kernel,
        out_shape=(
            jax.ShapeDtypeStruct((KSUP, KSUP // panels), jnp.float32),
            jax.ShapeDtypeStruct((SSEP, KSUP // panels), jnp.float32),
            jax.ShapeDtypeStruct((count * BLK, BLK), jnp.float32),
        ),
        in_specs=[SM, VM, VM, VM],
        out_specs=(VM, VM, VM),
        scratch_shapes=[
            pltpu.VMEM((rows, FRONT), jnp.bfloat16),
            pltpu.VMEM((FRONT, KSUP), jnp.float32),
            pltpu.VMEM((FRONT, 6 * BLK), jnp.bfloat16),
            pltpu.VMEM((FRONT, 6 * BLK), jnp.bfloat16),
            pltpu.VMEM((2 * BLK, SSEP), jnp.float32),
            pltpu.VMEM((BLK, BLK), jnp.float32),
            pltpu.VMEM((BLK, BLK), jnp.float32),
            pltpu.VMEM((1, FRONT), jnp.float32),
        ],
        compiler_params=pltpu.CompilerParams(vmem_limit_bytes=VMEM_LIMIT),
        name="leaf_front",
    )(subtree_of, design, touch, leaf_shift)
    whole, shifts = sum_blocks(blocks, separator_shift.reshape(2, BLK))
    result_rows = pl.pallas_call(
        separator_kernel,
        out_shape=jax.ShapeDtypeStruct((SSEP // leaves, SSEP // panels), jnp.float32),
        in_specs=[VM, VM],
        out_specs=VM,
        scratch_shapes=[
            pltpu.VMEM((SSEP, SSEP), jnp.float32),
            pltpu.VMEM((SSEP, 6 * BLK), jnp.bfloat16),
            pltpu.VMEM((SSEP, 6 * BLK), jnp.bfloat16),
            pltpu.VMEM((BLK, BLK), jnp.float32),
            pltpu.VMEM((BLK, BLK), jnp.float32),
        ],
        compiler_params=pltpu.CompilerParams(vmem_limit_bytes=VMEM_LIMIT),
        name="separator_front",
    )(whole, shifts)
    return (factor_cols, coupling_cols, result_rows)


def solution(mesh):
    placed = (P("leaf", "panel"), P(), P(), P(), P(), P("panel"))
    return jax.shard_map(
        per_device,
        mesh=mesh,
        in_specs=placed,
        out_specs=(P("leaf", "panel"), P("leaf", "panel"), P("leaf", "panel")),
        check_vma=False,
    )
```
